256 devices in a mesh: slab: 16 (over x_hi, y, core), batch: 16 (over x_lo, z).
Axes of the slice: x: 4 (x_hi: 2, x_lo: 2; x = x_hi * 2 + x_lo), y: 4, z: 8, core: 2. Of those that a mesh axis runs over, the one named last changes fastest.
Arguments:
- volumes: bfloat16 [256, 2, 16384], P('slab', None, 'batch'), may hold values from -6 to 6
- band_weights: bfloat16 [2, 1024, 32], P(None, 'slab'), may hold values from -1 to 1
- band_start: int32 [2, 1024], P(None, 'slab'), may hold values from 0 to 224
- images: bfloat16 [6144, 16384], P('batch'), may hold values from -7 to 7
- noise_precision: float32 [6144], P('batch'), may hold values from 0.005004883 to 0.050048828
- log_prior: float32 [2, 1024], P(None, 'slab'), may hold values from -4 to 4
Outputs:
- responsibilities: float32 [2, 1024, 6144], P(None, 'slab', 'batch')
- log_evidence: float32 [6144], P('batch')
- backprojection: float32 [256, 2, 16384], P('slab', None, 'batch')
The draws below stay inside these ranges and needn't reach their ends.
All inputs are finite; a program needn't handle non-finite values.
Results may differ from the reference program's by a relative error of at most 0.0069.
Values may be sent and summed in bfloat16 or wider, within the bound.
A program may use at most 64 MiB of HBM per device.

```python
import math
import jax
import jax.numpy as jnp
from jax import lax

K = 2
NZ = 256
P_SIZE = 16384
BAND = 32
O = 1024
N = 6144


def plane_field(key):
    field_key = jax.random.fold_in(key, 11)
    field = jnp.clip(jax.random.normal(field_key, (NZ, K, P_SIZE), jnp.float32), -6.0, 6.0)
    return field.astype(jnp.bfloat16)


def band_starts(key):
    base = jax.random.randint(jax.random.fold_in(key, 21), (K * O,), 0, NZ - BAND + 1)
    first = jax.random.randint(jax.random.fold_in(key, 22), (), 0, K * O)
    offset = jax.random.randint(jax.random.fold_in(key, 23), (), 1, K * O)
    second = (first + offset) % (K * O)
    slots = jnp.arange(K * O, dtype=jnp.int32)
    base = jnp.where(slots == first, NZ - BAND, base)
    base = jnp.where(slots == second, 0, base)
    return base.reshape(K, O).astype(jnp.int32)


def band_taps(key):
    sign_bits = jax.random.randint(jax.random.fold_in(key, 31), (K, O, BAND), 0, 2)
    signs = (2 * sign_bits - 1).astype(jnp.float32)
    ranks = jax.random.randint(jax.random.fold_in(key, 32), (K, O, BAND), 0, 1 << 20)
    ranks = ranks * BAND + jnp.arange(BAND, dtype=jnp.int32)
    order = jnp.argsort(ranks, axis=-1, stable=True)
    levels = jnp.sqrt(2.0 * jnp.arange(BAND, dtype=jnp.float32) + 1.0) / BAND
    return (signs * jnp.take(levels, order)).astype(jnp.bfloat16)


def draw_volumes(key, part):
    return plane_field(key)


def draw_band_weights(key, part):
    return band_taps(key)


def draw_band_start(key, part):
    return band_starts(key)


def draw_images(key, part):
    field = plane_field(key).reshape(NZ * K, P_SIZE)
    taps = band_taps(key).astype(jnp.float32).reshape(K * O, BAND)
    starts = band_starts(key).reshape(K * O)
    owner = jnp.arange(K * O, dtype=jnp.int32) // O

    def add_tap(tap, total):
        rows_index = (starts + tap) * K + owner
        picked = jnp.take(field, rows_index, axis=0).astype(jnp.float32)
        weight = lax.dynamic_slice_in_dim(taps, tap, 1, 1)
        return total + weight * picked
    signal = lax.fori_loop(0, BAND, add_tap, jnp.zeros((K * O, P_SIZE), jnp.float32))
    chosen = jax.random.randint(jax.random.fold_in(key, 41), (N,), 0, K * O)
    strength = jnp.exp(jax.random.uniform(jax.random.fold_in(key, 42), (N,), jnp.float32, math.log(0.02), math.log(0.06)))
    noise_key = jax.random.fold_in(key, 43)
    noise = jnp.clip(jax.random.normal(noise_key, (N, P_SIZE), jnp.float32), -6.0, 6.0)
    images = strength[:, None] * jnp.take(signal, chosen, axis=0) + noise
    return images.astype(jnp.bfloat16)


def steps_of(rng, shape, shards, smallest, top_value):
    def one(position, shards_of):
        steps = jax.random.uniform(jax.random.fold_in(jax.random.fold_in(rng, 6), position), (shards_of,), jnp.float32, smallest / len(shards), top_value / len(shards))
        return jnp.repeat(jnp.exp(steps), shape[position] // shards_of).reshape((-1,) + (1,) * (len(shape) - position - 1))

    level = one(*shards[0])
    for cut in shards[1:]:
        level = level * one(*cut)
    return level


def gaussian(key, dims, spread, most, split=(), kind=jnp.bfloat16):
    entries = spread * jax.random.normal(key, dims, jnp.float32)
    if split:
        entries = entries * steps_of(key, dims, split, -0.22, 0.18)
    return jnp.clip(entries, -most, most).astype(kind)


def setup_inputs(seed: int = 0) -> dict:
    key_of = jax.random.split(jax.random.key(seed), 7)
    volumes = draw_volumes(jax.random.fold_in(key_of[6], 71), 0)
    band_weights = draw_band_weights(jax.random.fold_in(key_of[6], 71), 0)
    band_start = draw_band_start(jax.random.fold_in(key_of[6], 71), 0)
    images = draw_images(jax.random.fold_in(key_of[6], 71), 0)
    noise_precision = jnp.clip(jnp.exp(math.log(0.050048828) - 2.3025851 * jax.random.uniform(key_of[4], (N,), jnp.float32) ** steps_of(key_of[4], (N,), ((0, 16),), -0.2, 0.2)), 0.005004883, 0.050048828)
    log_prior = gaussian(key_of[5], (K, O), 1.0, 4.0, ((1, 16),), jnp.float32)
    return dict(volumes=volumes, band_weights=band_weights, band_start=band_start, images=images, noise_precision=noise_precision, log_prior=log_prior)


def build_slice(band_weights, band_start, planes):
    offsets = planes[None, None, :] - band_start[:, :, None]
    taps = jnp.arange(BAND, dtype=jnp.int32)
    hits = offsets[..., None] == taps
    values = jnp.where(hits, band_weights.astype(jnp.float32)[:, :, None, :], jnp.float32(0.0))
    return jnp.sum(values, axis=-1)


def reference(volumes, band_weights, band_start, images, noise_precision, log_prior):
    slice_full = build_slice(band_weights, band_start, jnp.arange(NZ, dtype=jnp.int32))
    projection = jnp.einsum("koz,zkp->okp", slice_full, volumes.astype(jnp.float32)).astype(jnp.bfloat16)
    wide = projection.astype(jnp.float32)
    energy = jnp.sum(wide * wide, axis=2)
    flat = projection.reshape(O * K, P_SIZE)
    inner = jnp.dot(flat, images.T, preferred_element_type=jnp.float32).reshape(O, K, N)
    inner = jnp.transpose(inner, (1, 0, 2))
    score = noise_precision[None, None, :] * (inner - 0.5 * energy.T[:, :, None]) + log_prior[:, :, None]
    top = jnp.max(score, axis=(0, 1))
    total = jnp.sum(jnp.exp(score - top[None, None, :]), axis=(0, 1))
    log_evidence = top + jnp.log(total)
    responsibilities = jnp.exp(score - log_evidence[None, None, :])
    weights = responsibilities.astype(jnp.bfloat16).reshape(K * O, N)
    image_sum = jnp.dot(images.T, weights.T, preferred_element_type=jnp.float32).reshape(P_SIZE, K, O)
    backprojection = jnp.einsum("koz,pko->zkp", slice_full, image_sum, precision=lax.Precision.HIGHEST)
    return responsibilities, log_evidence, backprojection
```

```python
import functools

import jax
import jax.numpy as jnp
from jax import lax
from jax.experimental import pallas as pl
from jax.experimental.pallas import tpu as pltpu
from jax.sharding import PartitionSpec as P

F32, BF16 = jnp.float32, jnp.bfloat16
MESH = pl.DeviceIdType.MESH
SLABS, BATCHES, RING = 16, 16, 8
NT = (((1,), (1,)), ((), ()))
NN = (((1,), (0,)), ((), ()))


def dot(a, b, dims=NN):
    return lax.dot_general(a, b, dims, preferred_element_type=F32)


def in_three(x):
    first = x.astype(BF16).astype(F32)
    second = (x - first).astype(BF16).astype(F32)
    third = (x - first - second).astype(BF16).astype(F32)
    return first, second, third


def body(
    vol, pack, noise, images, resp_out, ev_out, back_out,
    img, vall, vslab, slices, acc, gout, gin, eout, ein, dout, din, noise_col,
    scores, rout, rin, wout, win, right_out, right_in, left_out, left_in, x_out, x_in,
    img_sem, vb_send, vb_recv, vs_send, vs_recv, sl_send, sl_recv, few_send, few_recv,
    red_send, red_recv,
):
    s, b = lax.axis_index("slab"), lax.axis_index("batch")
    xl, z = lax.div(b, RING), lax.rem(b, RING)
    rows, width = 32, 1024
    started = []

    def block(other, dz):
        return lax.rem(xl + other, 2) * RING + lax.rem(z + dz + RING, RING)

    def send(src, dst, to, send_sem, recv_sem):
        copy = pltpu.make_async_remote_copy(
            src_ref=src, dst_ref=dst, send_sem=send_sem, recv_sem=recv_sem,
            device_id=to, device_id_type=MESH,
        )
        copy.start()
        started.append(copy)

    def arrived(ref, send_sem, recv_sem):
        pltpu.make_async_remote_copy(
            src_ref=ref, dst_ref=ref, send_sem=send_sem, recv_sem=recv_sem,
            device_id=(s, b), device_id_type=MESH,
        ).wait_recv()

    order = [(0, 0), (1, 0)]
    for h in (1, 2, 3):
        order += [(0, -h), (0, h), (1, -h), (1, h)]
    order += [(0, 4), (1, 4)]

    def load(i):
        at = block(*order[i])
        return pltpu.make_async_copy(
            images.at[:, pl.ds(pl.multiple_of(at * width, width), width)],
            img.at[at], img_sem.at[i],
        )

    for i in range(16):
        load(i).start()

    barrier = pltpu.get_barrier_semaphore()
    for j in range(1, SLABS):
        pl.semaphore_signal(barrier, inc=1, device_id=(lax.rem(s + j, SLABS), b), device_id_type=MESH)
    for j in range(1, BATCHES):
        pl.semaphore_signal(barrier, inc=1, device_id=(s, lax.rem(b + j, BATCHES)), device_id_type=MESH)

    start = pack[:, 32:33]
    lane = lax.broadcasted_iota(jnp.int32, (128, 256), 1).astype(F32)
    offset = lane - start
    own = jnp.zeros((128, 256), F32)
    for t in range(32):
        own = jnp.where(offset == float(t), pack[:, t : t + 1], own)
    slices[s] = own.astype(BF16)
    vslab[:, pl.ds(pl.multiple_of(s * 16, 16), 16), :] = vol[...]
    prior_row = jnp.transpose(pack[...])[33:34, :]
    noise_col[...] = jnp.transpose(
        jnp.concatenate([noise[...], jnp.zeros((125, 128), F32)], axis=0)
    )

    pl.semaphore_wait(barrier, SLABS + BATCHES - 2)

    right = (s, block(0, 1))
    left = (s, block(0, -1))
    beside = (s, block(1, 0))
    twin_index = s + 1 - 2 * lax.rem(s, 2)
    twin = (twin_index, b)

    def ring(other, h, side):
        return (0 if side > 0 else 10) + 2 * h + other

    def forward(other, h, side, src):
        at = block(other, -h * side)
        dst = vall.at[at]
        if h == 3:
            half = pl.ds(0 if side > 0 else width // 2, width // 2)
            src, dst = src.at[:, :, half], dst.at[:, :, half]
        k = ring(other, h + 1, side)
        send(src, dst, right if side > 0 else left, vb_send.at[k], vb_recv.at[k])

    def take(other, h, side):
        at = block(other, -h * side)
        ref = vall.at[at]
        if h == 4:
            ref = ref.at[:, :, pl.ds(0 if side > 0 else width // 2, width // 2)]
        k = ring(other, h, side)
        arrived(ref, vb_send.at[k], vb_recv.at[k])

    forward(0, 0, 1, vol)
    forward(0, 0, -1, vol)
    send(vol, vall.at[b], beside, vb_send.at[0], vb_recv.at[0])

    def planes_of(index):
        return vslab.at[:, pl.ds(pl.multiple_of(index * 16, 16), 16), :]

    for j in range(1, 8):
        to = (lax.rem(s + 2 * j, SLABS), b)
        send(vol, planes_of(s), to, vs_send.at[j], vs_recv.at[j])
    send(vol, planes_of(s), twin, vs_send.at[8], vs_recv.at[8])
    for j in range(1, 8):
        to = (lax.rem(s + 2 * j, SLABS), b)
        send(slices.at[s], slices.at[s], to, sl_send.at[j], sl_recv.at[j])
    send(slices.at[s], slices.at[s], twin, sl_send.at[8], sl_recv.at[8])

    def multiply(i, ref):
        load(i).wait()
        part = dot(img[block(*order[i])], ref[...].reshape(rows, width), NT)
        if i == 0:
            acc[...] = part
        else:
            acc[...] += part

    multiply(0, vol)
    arrived(vall.at[block(1, 0)], vb_send.at[0], vb_recv.at[0])
    for side in (1, -1):
        forward(1, 0, side, vall.at[block(1, 0)])
    multiply(1, vall.at[block(1, 0)])

    def hop(h, first):
        i = first
        for other in (0, 1):
            for side in (1, -1):
                take(other, h, side)
                forward(other, h, side, vall.at[block(other, -h * side)])
            for side in (1, -1):
                multiply(i, vall.at[block(other, -h * side)])
                i += 1

    hop(1, 2)
    for j in range(1, 8):
        origin = lax.rem(s + SLABS - 2 * j, SLABS)
        arrived(planes_of(origin), vs_send.at[j], vs_recv.at[j])
        send(planes_of(origin), planes_of(origin), twin, vs_send.at[8 + j], vs_recv.at[8 + j])
    hop(2, 6)
    for j in range(1, 8):
        origin = lax.rem(s + SLABS - 2 * j, SLABS)
        arrived(slices.at[origin], sl_send.at[j], sl_recv.at[j])
        send(slices.at[origin], slices.at[origin], twin, sl_send.at[8 + j], sl_recv.at[8 + j])
    for j in range(8):
        origin = lax.rem(twin_index + SLABS - 2 * j, SLABS)
        arrived(planes_of(origin), vs_send.at[8 + j], vs_recv.at[8 + j])

    sums = []
    for k in range(2):
        projection = dot(slices[s, 64 * k : 64 * k + 64, :], vslab[k])
        sums.append(jnp.sum(projection * projection, axis=1, keepdims=True))
    energy = jnp.concatenate(sums, axis=0)
    energy = jnp.transpose(jnp.broadcast_to(energy, (128, 128)))[0:8, :]
    eout[...] = energy
    ein[b] = energy
    for j in range(1, BATCHES):
        to = (s, lax.rem(b + j, BATCHES))
        send(eout, ein.at[b], to, few_send.at[0], few_recv.at[0])

    hop(3, 10)

    arrived(ein.at[pl.ds(0, 15)], few_send.at[0], few_recv.at[0])
    energy = jnp.sum(ein[...], axis=0)
    line = lax.broadcasted_iota(jnp.int32, (8, 128), 0)
    energy = jnp.where(line == 1, prior_row, energy)
    dout[...] = energy
    din[s] = energy
    for j in range(1, SLABS):
        to = (lax.rem(s + j, SLABS), b)
        send(dout, din.at[s], to, few_send.at[1], few_recv.at[1])

    for other in (0, 1):
        for side in (1, -1):
            take(other, 4, side)
        multiply(14 + other, vall.at[block(other, 4)])

    packed = jnp.concatenate(
        [acc[0:128, :], acc[128:256, :], acc[256:384, :], jnp.zeros((128, 32), F32)], axis=1
    )
    gout[...] = packed.reshape(SLABS, 8, 128)
    gin[s] = gout[s]
    for j in range(1, SLABS):
        index = lax.rem(s + j, SLABS)
        send(gout.at[index], gin.at[s], (index, b), few_send.at[2], few_recv.at[2])

    for j in range(8):
        origin = lax.rem(twin_index + SLABS - 2 * j, SLABS)
        arrived(slices.at[origin], sl_send.at[8 + j], sl_recv.at[8 + j])
    arrived(din.at[pl.ds(0, 15)], few_send.at[1], few_recv.at[1])
    arrived(gin.at[pl.ds(0, 15)], few_send.at[2], few_recv.at[2])

    lane = lax.broadcasted_iota(jnp.int32, (8, 128), 1)
    slot = lax.div(lane, 16)
    stacked = []
    for k in range(2):
        groups = []
        for g in range(3):
            halves = []
            for half in range(2):
                tile = jnp.zeros((8, 128), F32)
                for i in range(8):
                    shift = (16 * i - 32 * g - 16 * k) % 128
                    piece = gin[8 * half + i]
                    piece = pltpu.roll(piece, shift, 1) if shift else piece
                    tile = jnp.where(slot == i, piece, tile)
                halves.append(tile)
            groups.append(jnp.concatenate(halves, axis=1))
        stacked += in_three(jnp.concatenate(groups, axis=0))
    stacked = jnp.concatenate(stacked, axis=0).astype(BF16)

    nz = jnp.concatenate(
        [noise_col[pl.ds(pl.multiple_of(s * 8, 8), 8), g : g + 1] for g in range(3)], axis=0
    )
    wide_lane = lax.broadcasted_iota(jnp.int32, (24, 256), 1)
    first_class = lax.rem(wide_lane, 128) < 64
    top = None
    for t in range(8):
        pair = slices[2 * t : 2 * t + 2].reshape(256, 256)
        both = dot(stacked, pair, NT)
        inner = jnp.where(
            first_class,
            both[0:24] + both[24:48] + both[48:72],
            both[72:96] + both[96:120] + both[120:144],
        )
        energy = jnp.concatenate([din[2 * t, 0:1, :], din[2 * t + 1, 0:1, :]], axis=1)
        prior = jnp.concatenate([din[2 * t, 1:2, :], din[2 * t + 1, 1:2, :]], axis=1)
        score = nz * (inner - 0.5 * energy) + prior
        scores[t] = score
        top = score if top is None else jnp.maximum(top, score)
    top = jnp.max(top, axis=1, keepdims=True)
    total = jnp.zeros((24, 256), F32)
    for t in range(8):
        total += jnp.exp(scores[t] - top)
    evidence = top + jnp.log(jnp.sum(total, axis=1, keepdims=True))
    spread = jnp.zeros((48, 256), F32)
    wide_evidence = jnp.broadcast_to(evidence, (24, 128))
    for t in range(8):
        posterior = jnp.exp(scores[t] - evidence)
        for side in range(2):
            rout[2 * t + side, 0:24, :] = posterior[:, 128 * side : 128 * side + 128]
            rout[2 * t + side, 24:48, :] = wide_evidence
        weight = jnp.concatenate(
            [jnp.where(first_class, posterior, 0.0), jnp.where(first_class, 0.0, posterior)], axis=0
        ).astype(BF16)
        spread += dot(weight, slices[2 * t : 2 * t + 2].reshape(256, 256))

    for i in range(SLABS):
        tile = jnp.zeros((8, 128), F32)
        for k in range(2):
            for g in range(3):
                at = 24 * k + 8 * g
                piece = spread[at : at + 8, 128 * (i // 8) : 128 * (i // 8) + 128]
                shift = (32 * g + 16 * k - 16 * (i % 8)) % 128
                piece = pltpu.roll(piece, shift, 1) if shift else piece
                tile = jnp.where(slot == 2 * g + k, piece, tile)
        wout[i] = tile
    win[s] = wout[s]
    for j in range(1, SLABS):
        index = lax.rem(s + j, SLABS)
        send(wout.at[index], win.at[s], (index, b), few_send.at[3], few_recv.at[3])
    rin[s] = rout[s]
    for j in range(1, SLABS):
        index = lax.rem(s + j, SLABS)
        send(rout.at[index], rin.at[s], (index, b), few_send.at[4], few_recv.at[4])

    arrived(win.at[pl.ds(0, 15)], few_send.at[3], few_recv.at[3])
    turned = jnp.transpose(win[...].reshape(128, 128))
    turned = jnp.concatenate([turned[0:32], turned[32:64], turned[64:96]], axis=1)
    high = turned.astype(BF16).astype(F32)
    low = turned - high
    planes = jnp.concatenate([high, low], axis=0).astype(BF16)

    def partial(other, dz):
        both = dot(planes, img[block(other, dz)])
        return both[0:rows] + both[rows : 2 * rows]

    half = width // 2
    for other in (0, 1):
        part = partial(other, 4).astype(BF16)
        for side, out, into, at in ((1, right_out, right_in, 0), (-1, left_out, left_in, half)):
            k = (0 if side > 0 else 8) + 2 * 3 + other
            out[other, 3, :, at : at + half] = part[:, at : at + half]
            cut = (slice(None), pl.ds(at, half))
            send(
                out.at[other, 3].at[cut], into.at[other, 3].at[cut],
                right if side > 0 else left, red_send.at[k], red_recv.at[k],
            )
    for h in (3, 2, 1):
        for other in (0, 1):
            for side, out, into, at in ((1, right_out, right_in, 0), (-1, left_out, left_in, half)):
                part = partial(other, side * h)
                k = (0 if side > 0 else 8) + 2 * h + other
                came = into.at[other, h]
                if h == 3:
                    came = came.at[:, pl.ds(at, half)]
                arrived(came, red_send.at[k], red_recv.at[k])
                if h == 3:
                    out[other, h - 1, :, :] = part.astype(BF16)
                    out[other, h - 1, :, at : at + half] = (
                        part[:, at : at + half] + came[...].astype(F32)
                    ).astype(BF16)
                else:
                    out[other, h - 1, :, :] = (part + came[...].astype(F32)).astype(BF16)
                k = (0 if side > 0 else 8) + 2 * (h - 1) + other
                send(
                    out.at[other, h - 1], into.at[other, h - 1],
                    right if side > 0 else left, red_send.at[k], red_recv.at[k],
                )

    arrived(rin.at[pl.ds(0, 15)], few_send.at[4], few_recv.at[4])
    for g in range(3):
        turned = rin[:, 8 * g : 8 * g + 8, :].reshape(128, 128)
        resp_out[:, 128 * g : 128 * g + 128] = jnp.transpose(turned)
        turned = rin[:, 24 + 8 * g : 32 + 8 * g, :].reshape(128, 128)
        ev_out[g : g + 1, :] = jnp.transpose(turned)[0:1, :]

    def last(other):
        part = partial(other, 0)
        for side, into in ((1, right_in), (-1, left_in)):
            k = (0 if side > 0 else 8) + other
            arrived(into.at[other, 0], red_send.at[k], red_recv.at[k])
            part += into[other, 0].astype(F32)
        return part

    x_out[...] = last(1).astype(BF16)
    send(x_out, x_in, beside, red_send.at[16], red_recv.at[16])
    mine = last(0)
    arrived(x_in, red_send.at[16], red_recv.at[16])
    back_out[...] = mine + x_in[...].astype(F32)

    for copy in started:
        copy.wait_send()


def local(volumes, band_weights, band_start, images, noise_precision, log_prior):
    planes, classes, width = volumes.shape
    owned = band_weights.shape[1]
    count, particles = classes * owned, images.shape[0]
    vol = jnp.swapaxes(volumes, 0, 1)
    pack = jnp.concatenate(
        [
            band_weights.reshape(count, -1).astype(F32),
            band_start.reshape(count, 1).astype(F32),
            log_prior.reshape(count, 1),
            jnp.zeros((count, 94), F32),
        ],
        axis=1,
    )
    vmem = pl.BlockSpec(memory_space=pltpu.VMEM)
    dma = pltpu.SemaphoreType.DMA
    few = (SLABS, 8, 128)
    responsibilities, log_evidence, back = pl.pallas_call(
        body,
        out_shape=(
            jax.ShapeDtypeStruct((count, particles), F32),
            jax.ShapeDtypeStruct((3, 128), F32),
            jax.ShapeDtypeStruct((classes * planes, width), F32),
        ),
        in_specs=[vmem, vmem, vmem, pl.BlockSpec(memory_space=pl.ANY)],
        out_specs=(vmem, vmem, vmem),
        scratch_shapes=[
            pltpu.VMEM((BATCHES, particles, width), BF16),
            pltpu.VMEM((BATCHES, classes, planes, width), BF16),
            pltpu.VMEM((classes, SLABS * planes, width), BF16),
            pltpu.VMEM((SLABS, count, SLABS * planes), BF16),
            pltpu.VMEM((particles, classes * planes), F32),
            pltpu.VMEM(few, F32),
            pltpu.VMEM(few, F32),
            pltpu.VMEM((8, 128), F32),
            pltpu.VMEM((BATCHES, 8, 128), F32),
            pltpu.VMEM((8, 128), F32),
            pltpu.VMEM(few, F32),
            pltpu.VMEM((128, 128), F32),
            pltpu.VMEM((8, 24, 256), F32),
            pltpu.VMEM((SLABS, 48, 128), F32),
            pltpu.VMEM((SLABS, 48, 128), F32),
            pltpu.VMEM(few, F32),
            pltpu.VMEM(few, F32),
            pltpu.VMEM((2, 4, 32, width), BF16),
            pltpu.VMEM((2, 4, 32, width), BF16),
            pltpu.VMEM((2, 4, 32, width), BF16),
            pltpu.VMEM((2, 4, 32, width), BF16),
            pltpu.VMEM((32, width), BF16),
            pltpu.VMEM((32, width), BF16),
            dma((16,)),
            dma((20,)), dma((20,)),
            dma((16,)), dma((16,)),
            dma((16,)), dma((16,)),
            dma((5,)), dma((5,)),
            dma((17,)), dma((17,)),
        ],
        compiler_params=pltpu.CompilerParams(
            collective_id=0, has_side_effects=True, vmem_limit_bytes=48 * 1024 * 1024
        ),
    )(vol, pack, noise_precision.reshape(3, 128), images)
    return (
        responsibilities.reshape(classes, owned, particles),
        log_evidence.reshape(particles),
        jnp.swapaxes(back.reshape(classes, planes, width), 0, 1),
    )


def solution(mesh):
    in_specs = (
        P("slab", None, "batch"),
        P(None, "slab", None),
        P(None, "slab"),
        P("batch", None),
        P("batch"),
        P(None, "slab"),
    )
    out_specs = (P(None, "slab", "batch"), P("batch"), P("slab", None, "batch"))
    return jax.shard_map(local, mesh=mesh, in_specs=in_specs, out_specs=out_specs, check_vma=False)
```

```python
import functools

import jax
import jax.numpy as jnp
from jax import lax
from jax.experimental import pallas as pl
from jax.experimental.pallas import tpu as pltpu
from jax.sharding import PartitionSpec as P

F32, BF16 = jnp.float32, jnp.bfloat16
MESH = pl.DeviceIdType.MESH
SLABS, BATCHES, RING = 16, 16, 8
NT = (((1,), (1,)), ((), ()))
NN = (((1,), (0,)), ((), ()))


def dot(a, b, dims=NN):
    return lax.dot_general(a, b, dims, preferred_element_type=F32)


def in_three(x):
    first = x.astype(BF16).astype(F32)
    second = (x - first).astype(BF16).astype(F32)
    third = (x - first - second).astype(BF16).astype(F32)
    return first, second, third


def body(
    vol_in, bands, starts, priors, noise, images, resp_out, ev_out, back_out,
    img, vol, vall, vslab, tables, slices, acc, gout, gin, eout, ein, prep,
    scores, rout, rin, wout, win, red_out, red_in, hold,
    img_sem, vb_send, vb_recv, vs_send, vs_recv, sl_send, sl_recv, few_send, few_recv,
    red_send, red_recv,
):
    s, b = lax.axis_index("slab"), lax.axis_index("batch")
    xl, z = lax.div(b, RING), lax.rem(b, RING)
    rows, width = 32, 1024
    started = []

    def block(other, dz):
        return lax.rem(xl + other, 2) * RING + lax.rem(z + dz + RING, RING)

    def send(src, dst, to, send_sem, recv_sem):
        copy = pltpu.make_async_remote_copy(
            src_ref=src, dst_ref=dst, send_sem=send_sem, recv_sem=recv_sem,
            device_id=to, device_id_type=MESH,
        )
        copy.start()
        started.append(copy)

    def arrived(ref, send_sem, recv_sem):
        pltpu.make_async_remote_copy(
            src_ref=ref, dst_ref=ref, send_sem=send_sem, recv_sem=recv_sem,
            device_id=(s, b), device_id_type=MESH,
        ).wait_recv()

    order = [(0, 0), (1, 0), (0, -1), (0, 1), (0, -2), (0, 2), (1, -1), (1, 1), (0, -3), (0, 3)]
    order += [(1, -2), (1, 2), (0, 4), (1, -3), (1, 3), (1, 4)]

    def load(i):
        at = block(*order[i])
        return pltpu.make_async_copy(
            images.at[:, pl.ds(pl.multiple_of(at * width, width), width)],
            img.at[at], img_sem.at[i],
        )

    for i in range(16):
        load(i).start()

    barrier = pltpu.get_barrier_semaphore()
    for j in range(1, SLABS):
        pl.semaphore_signal(barrier, inc=1, device_id=(lax.rem(s + j, SLABS), b), device_id_type=MESH)
    for j in range(1, BATCHES):
        pl.semaphore_signal(barrier, inc=1, device_id=(s, lax.rem(b + j, BATCHES)), device_id_type=MESH)

    for k in range(2):
        vol[k] = vol_in[:, k, :]
    vslab[:, pl.ds(pl.multiple_of(s * 16, 16), 16), :] = vol[...]

    tables[s, 0:32, :] = jnp.concatenate([bands[0], bands[1]], axis=1).astype(F32)
    tables[s, 32:33, :] = jnp.concatenate([starts[0:1, :], starts[1:2, :]], axis=1).astype(F32)
    tables[s, 33:34, :] = jnp.concatenate([priors[0:1, :], priors[1:2, :]], axis=1)
    tables[s, 34:40, :] = jnp.zeros((6, 128), F32)

    plane = lax.broadcasted_iota(jnp.int32, (128, 128), 1).astype(F32)

    def build(index):
        table = jnp.concatenate([tables[index], jnp.zeros((88, 128), F32)], axis=0)
        moved = jnp.transpose(table)
        start = jnp.broadcast_to(moved[:, 32:33], (128, 128))
        rest = jnp.where(start >= 128.0, start - 128.0, start)
        for step in (64, 32, 16, 8, 4, 2, 1):
            hit = rest >= float(step)
            moved = jnp.where(hit, pltpu.roll(moved, step, 1), moved)
            rest = jnp.where(hit, rest - float(step), rest)
        parts = []
        for first in (0.0, 128.0):
            offset = plane + first - start
            inside = jnp.logical_and(offset >= 0.0, offset < 32.0)
            parts.append(jnp.where(inside, moved, 0.0))
        slices[index] = jnp.concatenate(parts, axis=1).astype(BF16)

    def multiply(other, dz, ref):
        i = order.index((other, dz))
        load(i).wait()
        part = dot(img[block(other, dz)], ref[...].reshape(rows, width), NT)
        if i == 0:
            acc[...] = part
        else:
            acc[...] += part

    pl.semaphore_wait(barrier, SLABS + BATCHES - 2)

    right = (s, block(0, 1))
    left = (s, block(0, -1))
    beside = (s, block(1, 0))
    twin_index = s + 1 - 2 * lax.rem(s, 2)
    twin = (twin_index, b)

    half = width // 2
    ends = {1: 0, -1: half}

    near = {1: right, -1: left}
    far = {1: (s, block(0, 2)), -1: (s, block(0, -2))}

    def along(h, side):
        return 2 * (h - 1) + (side < 0)

    def across(h, side):
        return 8 if h == 0 else 7 + 2 * h + (side < 0)

    def part_of(other, ref):
        return ref.at[pl.ds(0, 1)] if other else ref

    def push(other, h, side, near_by, src=None):
        dst = vall.at[block(other, -side * (h - (1 if near_by else 2)))]
        src = part_of(other, dst if src is None else src)
        dst = part_of(other, dst)
        if h == 4:
            cut = pl.ds(ends[side], half)
            src, dst = src.at[:, :, cut], dst.at[:, :, cut]
        k = 16 * other + along(h, side)
        send(src, dst, (near if near_by else far)[side], vb_send.at[k], vb_recv.at[k])

    def take(other, h, side):
        ref = part_of(other, vall.at[block(other, -h * side)])
        if h == 4:
            ref = ref.at[:, :, pl.ds(ends[side], half)]
        k = 16 * other + along(h, side)
        arrived(ref, vb_send.at[k], vb_recv.at[k])

    def cross(h, side, src=None):
        k = across(h, side)
        dst = vall.at[block(0, -h * side)]
        src = dst if src is None else src
        if h:
            src, dst = src.at[pl.ds(1, 1)], dst.at[pl.ds(1, 1)]
        send(src, dst, beside, vb_send.at[k], vb_recv.at[k])

    def take_across(h, side):
        k = across(h, side)
        ref = vall.at[block(1, -h * side)]
        if h:
            ref = ref.at[pl.ds(1, 1)]
        arrived(ref, vb_send.at[k], vb_recv.at[k])

    for side in (1, -1):
        push(0, 2, side, False, vol)
    cross(0, 1, vol)
    for side in (1, -1):
        push(0, 1, side, True, vol)

    def planes_of(index):
        return vslab.at[:, pl.ds(pl.multiple_of(index * 16, 16), 16), :]

    for j in range(1, 8):
        to = (lax.rem(s + 2 * j, SLABS), b)
        send(vol, planes_of(s), to, vs_send.at[j], vs_recv.at[j])
    send(vol, planes_of(s), twin, vs_send.at[8], vs_recv.at[8])
    for j in range(1, 8):
        to = (lax.rem(s + 2 * j, SLABS), b)
        send(tables.at[s], tables.at[s], to, sl_send.at[j], sl_recv.at[j])
    send(tables.at[s], tables.at[s], twin, sl_send.at[8], sl_recv.at[8])

    def relay(ref, j, sends, recvs):
        arrived(ref, sends.at[j], recvs.at[j])
        send(ref, ref, twin, sends.at[8 + j], recvs.at[8 + j])

    def origin_of(index, j):
        return lax.rem(index + SLABS - 2 * j, SLABS)

    for g in range(3):
        prep[g : g + 1, :] = noise[pl.ds(128 * g, 128)].reshape(1, 128)
    prep[3:128, :] = jnp.zeros((125, 128), F32)
    prep[...] = jnp.transpose(prep[...])
    vslab[:, pl.ds(pl.multiple_of(s * 16, 16), 16), :] = vol[...]
    multiply(0, 0, vol)
    build(s)

    def stored(other, dz):
        multiply(other, dz, vall.at[block(other, dz)])

    def relay_far(other):
        for side in (1, -1):
            take(other, 2, side)
            push(other, 4, side, False)
            push(other, 3, side, True)

    take_across(0, 1)
    for side in (1, -1):
        push(1, 2, side, False)
    for side in (1, -1):
        push(1, 1, side, True)
    relay_far(0)
    for side in (1, -1):
        take(0, 1, side)
        cross(1, side)
    for side in (1, -1):
        cross(2, side)
    stored(1, 0)
    for dz in (-1, 1, -2, 2):
        stored(0, dz)
    for j in range(1, 8):
        relay(planes_of(origin_of(s, j)), j, vs_send, vs_recv)
    relay_far(1)
    for side in (1, -1):
        take(0, 3, side)
        cross(3, side)
    for side in (1, -1):
        take(0, 4, side)
    cross(4, 1)
    for side in (1, -1):
        take(1, 1, side)
        take_across(1, side)
        stored(1, -side)
    for j in range(8):
        origin = origin_of(twin_index, j)
        arrived(planes_of(origin), vs_send.at[8 + j], vs_recv.at[8 + j])

    sums = []
    for k in range(2):
        projection = dot(slices[s, 64 * k : 64 * k + 64, :], vslab[k])
        sums.append(jnp.sum(projection * projection, axis=1, keepdims=True))
    energy = jnp.concatenate(sums, axis=0)
    energy = jnp.transpose(jnp.broadcast_to(energy, (128, 128)))[0:8, :]
    eout[...] = energy
    ein[b] = energy
    for j in range(1, BATCHES):
        to = (s, lax.rem(b + j, BATCHES))
        send(eout, ein.at[b], to, few_send.at[0], few_recv.at[0])

    for j in range(1, 8):
        relay(tables.at[origin_of(s, j)], j, sl_send, sl_recv)
    for side in (1, -1):
        stored(0, -3 * side)
        take_across(2, side)
        stored(1, -2 * side)
    stored(0, 4)
    for j in range(1, 8):
        build(origin_of(s, j))
    for side in (1, -1):
        take(1, 3, side)
        take_across(3, side)
        stored(1, -3 * side)
    for side in (1, -1):
        take(1, 4, side)
    take_across(4, 1)
    stored(1, 4)

    arrived(ein.at[pl.ds(0, 15)], few_send.at[0], few_recv.at[0])
    energy = jnp.sum(ein[...], axis=0)

    packed = jnp.concatenate(
        [acc[0:128, :], acc[128:256, :], acc[256:384, :], jnp.zeros((128, 32), F32)], axis=1
    )
    gout[:, 0:8, :] = packed.reshape(SLABS, 8, 128)
    for i in range(SLABS):
        gout[i, 8:16, :] = energy
    gin[s] = gout[s]
    for j in range(1, SLABS):
        index = lax.rem(s + j, SLABS)
        send(gout.at[index], gin.at[s], (index, b), few_send.at[2], few_recv.at[2])

    for j in range(8):
        origin = origin_of(twin_index, j)
        arrived(tables.at[origin], sl_send.at[8 + j], sl_recv.at[8 + j])
        build(origin)
    arrived(gin.at[pl.ds(0, 15)], few_send.at[2], few_recv.at[2])

    lane = lax.broadcasted_iota(jnp.int32, (8, 128), 1)
    slot = lax.div(lane, 16)
    stacked = []
    for k in range(2):
        groups = []
        for g in range(3):
            halves = []
            for upper in range(2):
                tile = jnp.zeros((8, 128), F32)
                for i in range(8):
                    shift = (16 * i - 32 * g - 16 * k) % 128
                    piece = gin[8 * upper + i, 0:8, :]
                    piece = pltpu.roll(piece, shift, 1) if shift else piece
                    tile = jnp.where(slot == i, piece, tile)
                halves.append(tile)
            groups.append(jnp.concatenate(halves, axis=1))
        stacked += in_three(jnp.concatenate(groups, axis=0))
    stacked = jnp.concatenate(stacked, axis=0).astype(BF16)

    nz = jnp.concatenate(
        [prep[pl.ds(pl.multiple_of(s * 8, 8), 8), g : g + 1] for g in range(3)], axis=0
    )
    wide_lane = lax.broadcasted_iota(jnp.int32, (24, 256), 1)
    first_class = lax.rem(wide_lane, 128) < 64
    for t in range(8):
        both = dot(stacked, slices[2 * t : 2 * t + 2].reshape(256, 256), NT)
        scores[t] = jnp.where(
            first_class,
            both[0:24] + both[24:48] + both[48:72],
            both[72:96] + both[96:120] + both[120:144],
        )
    top = None
    for t in range(8):
        energy = jnp.concatenate([gin[2 * t, 8:9, :], gin[2 * t + 1, 8:9, :]], axis=1)
        prior = jnp.concatenate([tables[2 * t, 33:34, :], tables[2 * t + 1, 33:34, :]], axis=1)
        score = nz * (scores[t] - 0.5 * energy) + prior
        scores[t] = score
        top = score if top is None else jnp.maximum(top, score)
    top = jnp.max(top, axis=1, keepdims=True)
    total = jnp.zeros((24, 256), F32)
    for t in range(8):
        total += jnp.exp(scores[t] - top)
    evidence = top + jnp.log(jnp.sum(total, axis=1, keepdims=True))
    spread = jnp.zeros((48, 256), F32)
    wide_evidence = jnp.broadcast_to(evidence, (24, 128))
    for t in range(8):
        posterior = jnp.exp(scores[t] - evidence)
        for side in range(2):
            rout[2 * t + side, 0:24, :] = posterior[:, 128 * side : 128 * side + 128]
            rout[2 * t + side, 24:48, :] = wide_evidence
        weight = jnp.concatenate(
            [jnp.where(first_class, posterior, 0.0), jnp.where(first_class, 0.0, posterior)], axis=0
        ).astype(BF16)
        spread += dot(weight, slices[2 * t : 2 * t + 2].reshape(256, 256))

    for i in range(SLABS):
        tile = jnp.zeros((8, 128), F32)
        for k in range(2):
            for g in range(3):
                at = 24 * k + 8 * g
                piece = spread[at : at + 8, 128 * (i // 8) : 128 * (i // 8) + 128]
                shift = (32 * g + 16 * k - 16 * (i % 8)) % 128
                piece = pltpu.roll(piece, shift, 1) if shift else piece
                tile = jnp.where(slot == 2 * g + k, piece, tile)
        wout[i] = tile
    win[s] = wout[s]
    for j in range(1, SLABS):
        index = lax.rem(s + j, SLABS)
        send(wout.at[index], win.at[s], (index, b), few_send.at[3], few_recv.at[3])
    arrived(win.at[pl.ds(0, 15)], few_send.at[3], few_recv.at[3])
    rin[s] = rout[s]
    for j in range(1, SLABS):
        index = lax.rem(s + j, SLABS)
        send(rout.at[index], rin.at[s], (index, b), few_send.at[4], few_recv.at[4])

    turned = jnp.transpose(win[...].reshape(128, 128))
    turned = jnp.concatenate([turned[0:32], turned[32:64], turned[64:96]], axis=1)
    high = turned.astype(BF16).astype(F32)
    low = turned - high
    planes = jnp.concatenate([high, low], axis=0).astype(BF16)

    def partial(other, dz):
        both = dot(planes, img[block(other, dz)])
        return both[0:rows] + both[rows : 2 * rows]

    def region(ref, other, h, side):
        ref = ref.at[16 * other + along(h, side)]
        rows_of = pl.ds(0, 16 if other else 32)
        return ref.at[rows_of, pl.ds(ends[side], half)] if h == 4 else ref.at[rows_of]

    def pass_on(value, other, h, side, near_by):
        k = 16 * other + along(h, side)
        out, into = region(red_out, other, h, side), region(red_in, other, h, side)
        if h == 4:
            value = value[:, ends[side] : ends[side] + half]
        out[...] = value.astype(BF16)
        send(out, into, (near if near_by else far)[side], red_send.at[k], red_recv.at[k])

    def pass_across(value, k, first):
        cut = pl.ds(first, 16)
        out, into = red_out.at[k].at[cut], red_in.at[k].at[cut]
        out[...] = value.astype(BF16)
        send(out, into, beside, red_send.at[k], red_recv.at[k])

    def received(k, ref):
        arrived(ref, red_send.at[k], red_recv.at[k])
        return ref[...].astype(F32)

    def came(other, h, side):
        return received(16 * other + along(h, side), region(red_in, other, h, side))

    def split(h, side):
        part = partial(1, h * side)
        pass_across(part[16:32], across(h, side), 16)
        return part[0:16]

    def joined(h, side):
        k = across(h, side)
        part = partial(0, h * side)
        extra = received(k, red_in.at[k].at[pl.ds(16, 16)])
        return jnp.concatenate([part[0:16], part[16:32] + extra], axis=0)

    def gathered(part, other, side):
        at = ends[side]
        here = part[:, at : at + half] + came(other, 4, side)
        there = part[:, half - at : width - at]
        part = jnp.concatenate([here, there] if side > 0 else [there, here], axis=1)
        return part + came(other, 3, side)

    part = split(4, 1)
    for side in (1, -1):
        pass_on(part, 1, 4, side, False)
    for side in (1, -1):
        pass_on(split(3, side), 1, 3, side, True)
    part = joined(4, 1)
    for side in (1, -1):
        pass_on(part, 0, 4, side, False)
    for side in (1, -1):
        hold[(1 - side) // 2] = split(2, side)
    for side in (1, -1):
        pass_on(joined(3, side), 0, 3, side, True)
    for side in (1, -1):
        pass_on(gathered(hold[(1 - side) // 2], 1, side), 1, 2, side, False)
    for side in (1, -1):
        pass_on(split(1, side), 1, 1, side, True)
    hold[2] = split(0, 1)
    for side in (1, -1):
        pass_on(gathered(joined(2, side), 0, side), 0, 2, side, False)
    for side in (1, -1):
        pass_on(joined(1, side), 0, 1, side, True)
    part = hold[2]
    for h in (1, 2):
        for side in (1, -1):
            part += came(1, h, side)
    pass_across(part, 24, 0)

    arrived(rin.at[pl.ds(0, 15)], few_send.at[4], few_recv.at[4])
    for g in range(3):
        turned = rin[:, 8 * g : 8 * g + 8, :].reshape(128, 128)
        resp_out[:, 128 * g : 128 * g + 128] = jnp.transpose(turned)
        turned = rin[:, 24 + 8 * g : 32 + 8 * g, :].reshape(128, 128)
        ev_out[g : g + 1, :] = jnp.transpose(turned)[0:1, :]

    part = joined(0, 1)
    for h in (1, 2):
        for side in (1, -1):
            part += came(0, h, side)
    extra = received(24, red_in.at[24].at[pl.ds(0, 16)])
    part = jnp.concatenate([part[0:16] + extra, part[16:32]], axis=0)
    for k in range(2):
        back_out[:, k, :] = part[16 * k : 16 * k + 16]

    for copy in started:
        copy.wait_send()


def local(volumes, band_weights, band_start, images, noise_precision, log_prior):
    planes, classes, width = volumes.shape
    owned = band_weights.shape[1]
    count, particles = classes * owned, images.shape[0]
    vmem = pl.BlockSpec(memory_space=pltpu.VMEM)
    dma = pltpu.SemaphoreType.DMA
    few = (SLABS, 8, 128)
    responsibilities, log_evidence, back = pl.pallas_call(
        body,
        out_shape=(
            jax.ShapeDtypeStruct((count, particles), F32),
            jax.ShapeDtypeStruct((3, 128), F32),
            jax.ShapeDtypeStruct((planes, classes, width), F32),
        ),
        in_specs=[vmem] * 5 + [pl.BlockSpec(memory_space=pl.ANY)],
        out_specs=(vmem, vmem, vmem),
        scratch_shapes=[
            pltpu.VMEM((BATCHES, particles, width), BF16),
            pltpu.VMEM((classes, planes, width), BF16),
            pltpu.VMEM((BATCHES, classes, planes, width), BF16),
            pltpu.VMEM((classes, SLABS * planes, width), BF16),
            pltpu.VMEM((SLABS, 40, 128), F32),
            pltpu.VMEM((SLABS, count, SLABS * planes), BF16),
            pltpu.VMEM((particles, classes * planes), F32),
            pltpu.VMEM((SLABS, 16, 128), F32),
            pltpu.VMEM((SLABS, 16, 128), F32),
            pltpu.VMEM((8, 128), F32),
            pltpu.VMEM((BATCHES, 8, 128), F32),
            pltpu.VMEM((128, 128), F32),
            pltpu.VMEM((8, 24, 256), F32),
            pltpu.VMEM((SLABS, 48, 128), F32),
            pltpu.VMEM((SLABS, 48, 128), F32),
            pltpu.VMEM(few, F32),
            pltpu.VMEM(few, F32),
            pltpu.VMEM((25, 32, width), BF16),
            pltpu.VMEM((25, 32, width), BF16),
            pltpu.VMEM((3, 16, width), F32),
            dma((16,)),
            dma((24,)), dma((24,)),
            dma((16,)), dma((16,)),
            dma((16,)), dma((16,)),
            dma((5,)), dma((5,)),
            dma((25,)), dma((25,)),
        ],
        compiler_params=pltpu.CompilerParams(
            collective_id=0, has_side_effects=True, vmem_limit_bytes=48 * 1024 * 1024
        ),
    )(volumes, jnp.swapaxes(band_weights, 1, 2), band_start, log_prior, noise_precision, images)
    return (
        responsibilities.reshape(classes, owned, particles),
        log_evidence.reshape(particles),
        back,
    )


def solution(mesh):
    in_specs = (
        P("slab", None, "batch"),
        P(None, "slab", None),
        P(None, "slab"),
        P("batch", None),
        P("batch"),
        P(None, "slab"),
    )
    out_specs = (P(None, "slab", "batch"), P("batch"), P("slab", None, "batch"))
    return jax.shard_map(local, mesh=mesh, in_specs=in_specs, out_specs=out_specs, check_vma=False)
```

```python
import functools

import jax
import jax.numpy as jnp
from jax import lax
from jax.experimental import pallas as pl
from jax.experimental.pallas import tpu as pltpu
from jax.sharding import PartitionSpec as P

F32, BF16 = jnp.float32, jnp.bfloat16
MESH = pl.DeviceIdType.MESH
SLABS, BATCHES, RING = 16, 16, 8
NT = (((1,), (1,)), ((), ()))
NN = (((1,), (0,)), ((), ()))


def dot(a, b, dims=NN):
    return lax.dot_general(a, b, dims, preferred_element_type=F32)


def in_three(x):
    first = x.astype(BF16).astype(F32)
    second = (x - first).astype(BF16).astype(F32)
    third = (x - first - second).astype(BF16).astype(F32)
    return first, second, third


def body(
    vol_in, bands, starts, priors, noise, images, resp_out, ev_out, back_out,
    img, vol, vall, vslab, tables, slices, acc, gout, gin, eout, ein, prep,
    scores, rout, rin, wout, win, red_out, red_in, hold,
    img_sem, vb_send, vb_recv, vs_send, vs_recv, sl_send, sl_recv, few_send, few_recv,
    red_send, red_recv,
):
    s, b = lax.axis_index("slab"), lax.axis_index("batch")
    xl, z = lax.div(b, RING), lax.rem(b, RING)
    rows, width = 32, 1024
    started = []

    def block(other, dz):
        return lax.rem(xl + other, 2) * RING + lax.rem(z + dz + RING, RING)

    def send(src, dst, to, send_sem, recv_sem):
        copy = pltpu.make_async_remote_copy(
            src_ref=src, dst_ref=dst, send_sem=send_sem, recv_sem=recv_sem,
            device_id=to, device_id_type=MESH,
        )
        copy.start()
        started.append(copy)

    def arrived(ref, send_sem, recv_sem):
        pltpu.make_async_remote_copy(
            src_ref=ref, dst_ref=ref, send_sem=send_sem, recv_sem=recv_sem,
            device_id=(s, b), device_id_type=MESH,
        ).wait_recv()

    order = [(0, 0), (1, 0), (0, -1), (0, 1), (0, -2), (0, 2), (1, -1), (1, 1), (0, -3), (0, 3)]
    order += [(1, -2), (1, 2), (0, 4), (1, -3), (1, 3), (1, 4)]

    def load(i):
        at = block(*order[i])
        return pltpu.make_async_copy(
            images.at[:, pl.ds(pl.multiple_of(at * width, width), width)],
            img.at[at], img_sem.at[i],
        )

    for i in range(16):
        load(i).start()

    barrier = pltpu.get_barrier_semaphore()
    for j in range(1, SLABS):
        pl.semaphore_signal(barrier, inc=1, device_id=(lax.rem(s + j, SLABS), b), device_id_type=MESH)
    for other, dz in ((0, 1), (0, -1), (0, 2), (0, -2), (1, 0)):
        pl.semaphore_signal(barrier, inc=1, device_id=(s, block(other, dz)), device_id_type=MESH)
    for k in range(2):
        vol[k] = vol_in[:, k, :]
    vslab[:, pl.ds(pl.multiple_of(s * 16, 16), 16), :] = vol[...]

    tables[s, 0:32, :] = jnp.concatenate([bands[0], bands[1]], axis=1).astype(F32)
    tables[s, 32:33, :] = jnp.concatenate([starts[0:1, :], starts[1:2, :]], axis=1).astype(F32)
    tables[s, 33:34, :] = jnp.concatenate([priors[0:1, :], priors[1:2, :]], axis=1)
    tables[s, 34:40, :] = jnp.zeros((6, 128), F32)

    plane = lax.broadcasted_iota(jnp.int32, (128, 128), 1).astype(F32)

    def build(index):
        table = jnp.concatenate([tables[index], jnp.zeros((88, 128), F32)], axis=0)
        moved = jnp.transpose(table)
        start = jnp.broadcast_to(moved[:, 32:33], (128, 128))
        rest = jnp.where(start >= 128.0, start - 128.0, start)
        for step in (64, 32, 16, 8, 4, 2, 1):
            hit = rest >= float(step)
            moved = jnp.where(hit, pltpu.roll(moved, step, 1), moved)
            rest = jnp.where(hit, rest - float(step), rest)
        parts = []
        for first in (0.0, 128.0):
            offset = plane + first - start
            inside = jnp.logical_and(offset >= 0.0, offset < 32.0)
            parts.append(jnp.where(inside, moved, 0.0))
        slices[index] = jnp.concatenate(parts, axis=1).astype(BF16)

    def multiply(other, dz, ref):
        i = order.index((other, dz))
        load(i).wait()
        part = dot(img[block(other, dz)], ref[...].reshape(rows, width), NT)
        if i == 0:
            acc[...] = part
        else:
            acc[...] += part

    pl.semaphore_wait(barrier, SLABS + 4)

    right = (s, block(0, 1))
    left = (s, block(0, -1))
    beside = (s, block(1, 0))
    twin_index = s + 1 - 2 * lax.rem(s, 2)
    twin = (twin_index, b)

    half = width // 2
    ends = {1: 0, -1: half}

    near = {1: right, -1: left}
    far = {1: (s, block(0, 2)), -1: (s, block(0, -2))}

    def along(h, side):
        return 2 * (h - 1) + (side < 0)

    def across(h, side):
        return 8 if h == 0 else 7 + 2 * h + (side < 0)

    def part_of(other, ref):
        return ref.at[pl.ds(0, 1)] if other else ref

    def push(other, h, side, near_by, src=None):
        dst = vall.at[block(other, -side * (h - (1 if near_by else 2)))]
        src = part_of(other, dst if src is None else src)
        dst = part_of(other, dst)
        if h == 4:
            cut = pl.ds(ends[side], half)
            src, dst = src.at[:, :, cut], dst.at[:, :, cut]
        k = 16 * other + along(h, side)
        send(src, dst, (near if near_by else far)[side], vb_send.at[k], vb_recv.at[k])

    def take(other, h, side):
        ref = part_of(other, vall.at[block(other, -h * side)])
        if h == 4:
            ref = ref.at[:, :, pl.ds(ends[side], half)]
        k = 16 * other + along(h, side)
        arrived(ref, vb_send.at[k], vb_recv.at[k])

    def cross(h, side, src=None):
        k = across(h, side)
        dst = vall.at[block(0, -h * side)]
        src = dst if src is None else src
        if h:
            src, dst = src.at[pl.ds(1, 1)], dst.at[pl.ds(1, 1)]
        send(src, dst, beside, vb_send.at[k], vb_recv.at[k])

    def take_across(h, side):
        k = across(h, side)
        ref = vall.at[block(1, -h * side)]
        if h:
            ref = ref.at[pl.ds(1, 1)]
        arrived(ref, vb_send.at[k], vb_recv.at[k])

    for side in (1, -1):
        push(0, 2, side, False, vol)
    cross(0, 1, vol)
    for side in (1, -1):
        push(0, 1, side, True, vol)

    def planes_of(index):
        return vslab.at[:, pl.ds(pl.multiple_of(index * 16, 16), 16), :]

    def slab_of(index, opposite, steps):
        half_x = lax.rem(lax.div(index, 8) + opposite, 2)
        y = lax.rem(lax.div(lax.rem(index, 8), 2) + steps + 4, 4)
        return 8 * half_x + 2 * y + lax.rem(index, 2)

    def origin_of(index, j):
        return slab_of(index, 1, 4 - j) if j >= 4 else slab_of(index, 0, -j)

    def spread_own(src, dst, sends, recvs):
        send(src, dst, (slab_of(s, 1, 0), b), sends.at[4], recvs.at[4])
        for j in (1, 2, 3):
            send(src, dst, (slab_of(s, 0, j), b), sends.at[j], recvs.at[j])
        send(src, dst, twin, sends.at[8], recvs.at[8])

    def relay(ref, j, sends, recvs):
        arrived(ref, sends.at[j], recvs.at[j])
        if j == 4:
            for i in (1, 2, 3):
                send(ref, ref, (slab_of(s, 0, i), b), sends.at[4 + i], recvs.at[4 + i])
        send(ref, ref, twin, sends.at[8 + j], recvs.at[8 + j])

    spread_own(vol, planes_of(s), vs_send, vs_recv)
    spread_own(tables.at[s], tables.at[s], sl_send, sl_recv)

    for g in range(3):
        prep[g : g + 1, :] = noise[pl.ds(128 * g, 128)].reshape(1, 128)
    prep[3:128, :] = jnp.zeros((125, 128), F32)
    prep[...] = jnp.transpose(prep[...])
    vslab[:, pl.ds(pl.multiple_of(s * 16, 16), 16), :] = vol[...]
    multiply(0, 0, vol)
    build(s)

    def stored(other, dz):
        multiply(other, dz, vall.at[block(other, dz)])

    def relay_far(other):
        for side in (1, -1):
            take(other, 2, side)
            push(other, 4, side, False)
            push(other, 3, side, True)

    take_across(0, 1)
    for side in (1, -1):
        push(1, 2, side, False)
    for side in (1, -1):
        push(1, 1, side, True)
    relay_far(0)
    for side in (1, -1):
        take(0, 1, side)
        cross(1, side)
    for side in (1, -1):
        cross(2, side)
    relay(planes_of(origin_of(s, 4)), 4, vs_send, vs_recv)
    relay(tables.at[origin_of(s, 4)], 4, sl_send, sl_recv)
    stored(1, 0)
    for dz in (-1, 1, -2, 2):
        stored(0, dz)
    for j in (1, 2, 3, 5, 6, 7):
        relay(planes_of(origin_of(s, j)), j, vs_send, vs_recv)
    relay_far(1)
    for side in (1, -1):
        take(0, 3, side)
        cross(3, side)
    for side in (1, -1):
        take(0, 4, side)
    cross(4, 1)
    for side in (1, -1):
        take(1, 1, side)
        take_across(1, side)
        stored(1, -side)
    for j in range(8):
        origin = origin_of(twin_index, j)
        arrived(planes_of(origin), vs_send.at[8 + j], vs_recv.at[8 + j])

    sums = []
    for k in range(2):
        projection = dot(slices[s, 64 * k : 64 * k + 64, :], vslab[k])
        sums.append(jnp.sum(projection * projection, axis=1, keepdims=True))
    energy = jnp.concatenate(sums, axis=0)
    energy = jnp.transpose(jnp.broadcast_to(energy, (128, 128)))[0:8, :]
    eout[0] = energy
    ein[z] = energy
    for j in range(1, RING):
        send(eout.at[0], ein.at[z], (s, block(0, j)), few_send.at[0], few_recv.at[0])

    for j in (1, 2, 3, 5, 6, 7):
        relay(tables.at[origin_of(s, j)], j, sl_send, sl_recv)
    for side in (1, -1):
        stored(0, -3 * side)
        take_across(2, side)
        stored(1, -2 * side)
    stored(0, 4)
    for j in range(1, 8):
        build(origin_of(s, j))
    arrived(ein.at[pl.ds(0, RING - 1)], few_send.at[0], few_recv.at[0])
    eout[1] = jnp.sum(ein[0:RING], axis=0)
    send(eout.at[1], ein.at[RING], beside, few_send.at[1], few_recv.at[1])
    for side in (1, -1):
        take(1, 3, side)
        take_across(3, side)
        stored(1, -3 * side)
    for side in (1, -1):
        take(1, 4, side)
    take_across(4, 1)
    stored(1, 4)
    arrived(ein.at[RING], few_send.at[1], few_recv.at[1])
    energy = eout[1] + ein[RING]

    packed = jnp.concatenate(
        [acc[0:128, :], acc[128:256, :], acc[256:384, :], jnp.zeros((128, 32), F32)], axis=1
    )
    gout[:, 0:8, :] = packed.reshape(SLABS, 8, 128)
    for i in range(SLABS):
        gout[i, 8:16, :] = energy
    gin[s] = gout[s]
    for j in range(1, SLABS):
        index = lax.rem(s + j, SLABS)
        send(gout.at[index], gin.at[s], (index, b), few_send.at[2], few_recv.at[2])

    for j in range(8):
        origin = origin_of(twin_index, j)
        arrived(tables.at[origin], sl_send.at[8 + j], sl_recv.at[8 + j])
        build(origin)
    arrived(gin.at[pl.ds(0, 15)], few_send.at[2], few_recv.at[2])

    lane = lax.broadcasted_iota(jnp.int32, (8, 128), 1)
    slot = lax.div(lane, 16)
    stacked = []
    for k in range(2):
        groups = []
        for g in range(3):
            halves = []
            for upper in range(2):
                tile = jnp.zeros((8, 128), F32)
                for i in range(8):
                    shift = (16 * i - 32 * g - 16 * k) % 128
                    piece = gin[8 * upper + i, 0:8, :]
                    piece = pltpu.roll(piece, shift, 1) if shift else piece
                    tile = jnp.where(slot == i, piece, tile)
                halves.append(tile)
            groups.append(jnp.concatenate(halves, axis=1))
        stacked += in_three(jnp.concatenate(groups, axis=0))
    stacked = jnp.concatenate(stacked, axis=0).astype(BF16)

    nz = jnp.concatenate(
        [prep[pl.ds(pl.multiple_of(s * 8, 8), 8), g : g + 1] for g in range(3)], axis=0
    )
    wide_lane = lax.broadcasted_iota(jnp.int32, (24, 256), 1)
    first_class = lax.rem(wide_lane, 128) < 64
    for t in range(8):
        both = dot(stacked, slices[2 * t : 2 * t + 2].reshape(256, 256), NT)
        scores[t] = jnp.where(
            first_class,
            both[0:24] + both[24:48] + both[48:72],
            both[72:96] + both[96:120] + both[120:144],
        )
    top = None
    for t in range(8):
        energy = jnp.concatenate([gin[2 * t, 8:9, :], gin[2 * t + 1, 8:9, :]], axis=1)
        prior = jnp.concatenate([tables[2 * t, 33:34, :], tables[2 * t + 1, 33:34, :]], axis=1)
        score = nz * (scores[t] - 0.5 * energy) + prior
        scores[t] = score
        top = score if top is None else jnp.maximum(top, score)
    top = jnp.max(top, axis=1, keepdims=True)
    total = jnp.zeros((24, 256), F32)
    for t in range(8):
        total += jnp.exp(scores[t] - top)
    evidence = top + jnp.log(jnp.sum(total, axis=1, keepdims=True))
    spread = jnp.zeros((48, 256), F32)
    column = lax.broadcasted_iota(jnp.int32, (8, 128), 1)
    tile = jnp.zeros((8, 128), F32)
    for g in range(3):
        tile = jnp.where(column == g, evidence[8 * g : 8 * g + 8], tile)
    for t in range(8):
        posterior = jnp.exp(scores[t] - evidence)
        for side in range(2):
            rout[2 * t + side, 0:24, :] = posterior[:, 128 * side : 128 * side + 128]
            rout[2 * t + side, 24:32, :] = tile
        weight = jnp.concatenate(
            [jnp.where(first_class, posterior, 0.0), jnp.where(first_class, 0.0, posterior)], axis=0
        ).astype(BF16)
        spread += dot(weight, slices[2 * t : 2 * t + 2].reshape(256, 256))

    for i in range(SLABS):
        tile = jnp.zeros((8, 128), F32)
        for k in range(2):
            for g in range(3):
                at = 24 * k + 8 * g
                piece = spread[at : at + 8, 128 * (i // 8) : 128 * (i // 8) + 128]
                shift = (32 * g + 16 * k - 16 * (i % 8)) % 128
                piece = pltpu.roll(piece, shift, 1) if shift else piece
                tile = jnp.where(slot == 2 * g + k, piece, tile)
        wout[i] = tile
    win[s] = wout[s]
    for j in range(1, SLABS):
        index = lax.rem(s + j, SLABS)
        send(wout.at[index], win.at[s], (index, b), few_send.at[3], few_recv.at[3])
    arrived(win.at[pl.ds(0, 15)], few_send.at[3], few_recv.at[3])
    turned = jnp.transpose(win[...].reshape(128, 128))
    turned = jnp.concatenate([turned[0:32], turned[32:64], turned[64:96]], axis=1)
    high = turned.astype(BF16).astype(F32)
    low = turned - high
    planes = jnp.concatenate([high, low], axis=0).astype(BF16)

    def partial(other, dz):
        both = dot(planes, img[block(other, dz)])
        return both[0:rows] + both[rows : 2 * rows]

    def region(ref, other, h, side):
        ref = ref.at[16 * other + along(h, side)]
        rows_of = pl.ds(0, 16 if other else 32)
        return ref.at[rows_of, pl.ds(ends[side], half)] if h == 4 else ref.at[rows_of]

    def pass_on(value, other, h, side, near_by):
        k = 16 * other + along(h, side)
        out, into = region(red_out, other, h, side), region(red_in, other, h, side)
        if h == 4:
            value = value[:, ends[side] : ends[side] + half]
        out[...] = value.astype(BF16)
        send(out, into, (near if near_by else far)[side], red_send.at[k], red_recv.at[k])

    def pass_across(value, k, first):
        cut = pl.ds(first, 16)
        out, into = red_out.at[k].at[cut], red_in.at[k].at[cut]
        out[...] = value.astype(BF16)
        send(out, into, beside, red_send.at[k], red_recv.at[k])

    def received(k, ref):
        arrived(ref, red_send.at[k], red_recv.at[k])
        return ref[...].astype(F32)

    def came(other, h, side):
        return received(16 * other + along(h, side), region(red_in, other, h, side))

    def split(h, side):
        part = partial(1, h * side)
        pass_across(part[16:32], across(h, side), 16)
        return part[0:16]

    def joined(h, side):
        k = across(h, side)
        part = partial(0, h * side)
        extra = received(k, red_in.at[k].at[pl.ds(16, 16)])
        return jnp.concatenate([part[0:16], part[16:32] + extra], axis=0)

    def gathered(part, other, side):
        at = ends[side]
        here = part[:, at : at + half] + came(other, 4, side)
        there = part[:, half - at : width - at]
        part = jnp.concatenate([here, there] if side > 0 else [there, here], axis=1)
        return part + came(other, 3, side)

    part = split(4, 1)
    for side in (1, -1):
        pass_on(part, 1, 4, side, False)
    for side in (1, -1):
        pass_on(split(3, side), 1, 3, side, True)
    part = joined(4, 1)
    for side in (1, -1):
        pass_on(part, 0, 4, side, False)
    for side in (1, -1):
        hold[(1 - side) // 2] = split(2, side)
    for side in (1, -1):
        pass_on(joined(3, side), 0, 3, side, True)
    for side in (1, -1):
        pass_on(gathered(hold[(1 - side) // 2], 1, side), 1, 2, side, False)
    for side in (1, -1):
        pass_on(split(1, side), 1, 1, side, True)
    hold[2] = split(0, 1)
    rin[s] = rout[s]
    for j in range(1, SLABS):
        index = lax.rem(s + j, SLABS)
        send(rout.at[index], rin.at[s], (index, b), few_send.at[4], few_recv.at[4])
    for side in (1, -1):
        pass_on(gathered(joined(2, side), 0, side), 0, 2, side, False)
    for side in (1, -1):
        pass_on(joined(1, side), 0, 1, side, True)
    part = hold[2]
    for h in (1, 2):
        for side in (1, -1):
            part += came(1, h, side)
    pass_across(part, 24, 0)

    arrived(rin.at[pl.ds(0, 15)], few_send.at[4], few_recv.at[4])
    for g in range(3):
        turned = rin[:, 8 * g : 8 * g + 8, :].reshape(128, 128)
        resp_out[:, 128 * g : 128 * g + 128] = jnp.transpose(turned)
    ev_out[...] = jnp.transpose(rin[:, 24:32, :].reshape(128, 128))[0:3, :]

    part = joined(0, 1)
    for h in (1, 2):
        for side in (1, -1):
            part += came(0, h, side)
    extra = received(24, red_in.at[24].at[pl.ds(0, 16)])
    part = jnp.concatenate([part[0:16] + extra, part[16:32]], axis=0)
    for k in range(2):
        back_out[:, k, :] = part[16 * k : 16 * k + 16]

    for copy in started:
        copy.wait_send()


def local(volumes, band_weights, band_start, images, noise_precision, log_prior):
    planes, classes, width = volumes.shape
    owned = band_weights.shape[1]
    count, particles = classes * owned, images.shape[0]
    vmem = pl.BlockSpec(memory_space=pltpu.VMEM)
    dma = pltpu.SemaphoreType.DMA
    few = (SLABS, 8, 128)
    responsibilities, log_evidence, back = pl.pallas_call(
        body,
        out_shape=(
            jax.ShapeDtypeStruct((count, particles), F32),
            jax.ShapeDtypeStruct((3, 128), F32),
            jax.ShapeDtypeStruct((planes, classes, width), F32),
        ),
        in_specs=[vmem] * 5 + [pl.BlockSpec(memory_space=pl.ANY)],
        out_specs=(vmem, vmem, vmem),
        scratch_shapes=[
            pltpu.VMEM((BATCHES, particles, width), BF16),
            pltpu.VMEM((classes, planes, width), BF16),
            pltpu.VMEM((BATCHES, classes, planes, width), BF16),
            pltpu.VMEM((classes, SLABS * planes, width), BF16),
            pltpu.VMEM((SLABS, 40, 128), F32),
            pltpu.VMEM((SLABS, count, SLABS * planes), BF16),
            pltpu.VMEM((particles, classes * planes), F32),
            pltpu.VMEM((SLABS, 16, 128), F32),
            pltpu.VMEM((SLABS, 16, 128), F32),
            pltpu.VMEM((2, 8, 128), F32),
            pltpu.VMEM((RING + 1, 8, 128), F32),
            pltpu.VMEM((128, 128), F32),
            pltpu.VMEM((8, 24, 256), F32),
            pltpu.VMEM((SLABS, 32, 128), F32),
            pltpu.VMEM((SLABS, 32, 128), F32),
            pltpu.VMEM(few, F32),
            pltpu.VMEM(few, F32),
            pltpu.VMEM((25, 32, width), BF16),
            pltpu.VMEM((25, 32, width), BF16),
            pltpu.VMEM((3, 16, width), F32),
            dma((16,)),
            dma((24,)), dma((24,)),
            dma((16,)), dma((16,)),
            dma((16,)), dma((16,)),
            dma((5,)), dma((5,)),
            dma((25,)), dma((25,)),
        ],
        compiler_params=pltpu.CompilerParams(
            collective_id=0, has_side_effects=True, vmem_limit_bytes=48 * 1024 * 1024
        ),
    )(volumes, jnp.swapaxes(band_weights, 1, 2), band_start, log_prior, noise_precision, images)
    return (
        responsibilities.reshape(classes, owned, particles),
        log_evidence.reshape(particles),
        back,
    )


def solution(mesh):
    in_specs = (
        P("slab", None, "batch"),
        P(None, "slab", None),
        P(None, "slab"),
        P("batch", None),
        P("batch"),
        P(None, "slab"),
    )
    out_specs = (P(None, "slab", "batch"), P("batch"), P("slab", None, "batch"))
    return jax.shard_map(local, mesh=mesh, in_specs=in_specs, out_specs=out_specs, check_vma=False)
```

```python
import functools

import jax
import jax.numpy as jnp
from jax import lax
from jax.experimental import pallas as pl
from jax.experimental.pallas import tpu as pltpu
from jax.sharding import PartitionSpec as P

F32, BF16 = jnp.float32, jnp.bfloat16
MESH = pl.DeviceIdType.MESH
SLABS, BATCHES, RING = 16, 16, 8
NT = (((1,), (1,)), ((), ()))
NN = (((1,), (0,)), ((), ()))


def dot(a, b, dims=NN):
    return lax.dot_general(a, b, dims, preferred_element_type=F32)


def in_three(x):
    first = x.astype(BF16).astype(F32)
    second = (x - first).astype(BF16).astype(F32)
    third = (x - first - second).astype(BF16).astype(F32)
    return first, second, third


def body(
    vol_hbm, bands_hbm, starts_hbm, priors_hbm, noise_hbm, images, resp_out, ev_out, back_out,
    vol_in, bands, starts, priors, noise, img, vol, vall, vslab, tables, slices, acc, gout, gin, eout, ein, prep,
    scores, rout, rin, wout, win, red_out, red_in, hold,
    img_sem, vb_send, vb_recv, vs_send, vs_recv, sl_send, sl_recv, few_send, few_recv,
    red_send, red_recv,
):
    s, b = lax.axis_index("slab"), lax.axis_index("batch")
    xl, z = lax.div(b, RING), lax.rem(b, RING)
    rows, width = 32, 1024
    started = []

    def block(other, dz):
        return lax.rem(xl + other, 2) * RING + lax.rem(z + dz + RING, RING)

    def send(src, dst, to, send_sem, recv_sem):
        copy = pltpu.make_async_remote_copy(
            src_ref=src, dst_ref=dst, send_sem=send_sem, recv_sem=recv_sem,
            device_id=to, device_id_type=MESH,
        )
        copy.start()
        started.append(copy)

    def arrived(ref, send_sem, recv_sem):
        pltpu.make_async_remote_copy(
            src_ref=ref, dst_ref=ref, send_sem=send_sem, recv_sem=recv_sem,
            device_id=(s, b), device_id_type=MESH,
        ).wait_recv()

    order = [(0, 0), (1, 0), (0, -1), (0, 1), (0, -2), (0, 2), (1, -1), (1, 1), (0, -3), (0, 3)]
    order += [(1, -2), (1, 2), (0, 4), (1, -3), (1, 3), (1, 4)]

    def load(i):
        at = block(*order[i])
        return pltpu.make_async_copy(
            images.at[:, pl.ds(pl.multiple_of(at * width, width), width)],
            img.at[at], img_sem.at[i],
        )

    small = [
        pltpu.make_async_copy(src, dst, img_sem.at[16 + i])
        for i, (src, dst) in enumerate(
            (
                (vol_hbm, vol_in), (bands_hbm, bands), (starts_hbm, starts),
                (priors_hbm, priors), (noise_hbm, noise),
            )
        )
    ]
    for copy in small:
        copy.start()
    for i in range(16):
        load(i).start()

    barrier = pltpu.get_barrier_semaphore()
    for j in range(1, SLABS):
        pl.semaphore_signal(barrier, inc=1, device_id=(lax.rem(s + j, SLABS), b), device_id_type=MESH)
    for other, dz in ((0, 1), (0, -1), (0, 2), (0, -2), (1, 0)):
        pl.semaphore_signal(barrier, inc=1, device_id=(s, block(other, dz)), device_id_type=MESH)
    for copy in small:
        copy.wait()
    for k in range(2):
        vol[k] = vol_in[:, k, :]
    vslab[:, pl.ds(pl.multiple_of(s * 16, 16), 16), :] = vol[...]

    tables[s, 0:32, :] = jnp.concatenate([bands[0], bands[1]], axis=1).astype(F32)
    tables[s, 32:33, :] = jnp.concatenate([starts[0:1, :], starts[1:2, :]], axis=1).astype(F32)
    tables[s, 33:34, :] = jnp.concatenate([priors[0:1, :], priors[1:2, :]], axis=1)
    tables[s, 34:40, :] = jnp.zeros((6, 128), F32)

    plane = lax.broadcasted_iota(jnp.int32, (128, 128), 1).astype(F32)

    def build(index):
        table = jnp.concatenate([tables[index], jnp.zeros((88, 128), F32)], axis=0)
        moved = jnp.transpose(table)
        start = jnp.broadcast_to(moved[:, 32:33], (128, 128))
        rest = jnp.where(start >= 128.0, start - 128.0, start)
        for step in (64, 32, 16, 8, 4, 2, 1):
            hit = rest >= float(step)
            moved = jnp.where(hit, pltpu.roll(moved, step, 1), moved)
            rest = jnp.where(hit, rest - float(step), rest)
        parts = []
        for first in (0.0, 128.0):
            offset = plane + first - start
            inside = jnp.logical_and(offset >= 0.0, offset < 32.0)
            parts.append(jnp.where(inside, moved, 0.0))
        slices[index] = jnp.concatenate(parts, axis=1).astype(BF16)

    def multiply(other, dz, ref):
        i = order.index((other, dz))
        load(i).wait()
        part = dot(img[block(other, dz)], ref[...].reshape(rows, width), NT)
        if i == 0:
            acc[...] = part
        else:
            acc[...] += part

    pl.semaphore_wait(barrier, SLABS + 4)

    right = (s, block(0, 1))
    left = (s, block(0, -1))
    beside = (s, block(1, 0))
    twin_index = s + 1 - 2 * lax.rem(s, 2)
    twin = (twin_index, b)

    half = width // 2
    ends = {1: 0, -1: half}

    near = {1: right, -1: left}
    far = {1: (s, block(0, 2)), -1: (s, block(0, -2))}

    def along(h, side):
        return 2 * (h - 1) + (side < 0)

    def across(h, side):
        return 8 if h == 0 else 7 + 2 * h + (side < 0)

    def part_of(other, ref):
        return ref.at[pl.ds(0, 1)] if other else ref

    def push(other, h, side, near_by, src=None):
        dst = vall.at[block(other, -side * (h - (1 if near_by else 2)))]
        src = part_of(other, dst if src is None else src)
        dst = part_of(other, dst)
        if h == 4:
            cut = pl.ds(ends[side], half)
            src, dst = src.at[:, :, cut], dst.at[:, :, cut]
        k = 16 * other + along(h, side)
        send(src, dst, (near if near_by else far)[side], vb_send.at[k], vb_recv.at[k])

    def take(other, h, side):
        ref = part_of(other, vall.at[block(other, -h * side)])
        if h == 4:
            ref = ref.at[:, :, pl.ds(ends[side], half)]
        k = 16 * other + along(h, side)
        arrived(ref, vb_send.at[k], vb_recv.at[k])

    def cross(h, side, src=None):
        k = across(h, side)
        dst = vall.at[block(0, -h * side)]
        src = dst if src is None else src
        if h:
            src, dst = src.at[pl.ds(1, 1)], dst.at[pl.ds(1, 1)]
        send(src, dst, beside, vb_send.at[k], vb_recv.at[k])

    def take_across(h, side):
        k = across(h, side)
        ref = vall.at[block(1, -h * side)]
        if h:
            ref = ref.at[pl.ds(1, 1)]
        arrived(ref, vb_send.at[k], vb_recv.at[k])

    for side in (1, -1):
        push(0, 2, side, False, vol)
    cross(0, 1, vol)
    for side in (1, -1):
        push(0, 1, side, True, vol)

    def planes_of(index):
        return vslab.at[:, pl.ds(pl.multiple_of(index * 16, 16), 16), :]

    def slab_of(index, opposite, steps):
        half_x = lax.rem(lax.div(index, 8) + opposite, 2)
        y = lax.rem(lax.div(lax.rem(index, 8), 2) + steps + 4, 4)
        return 8 * half_x + 2 * y + lax.rem(index, 2)

    def origin_of(index, j):
        return slab_of(index, 1, 4 - j) if j >= 4 else slab_of(index, 0, -j)

    def spread_own(src, dst, sends, recvs):
        send(src, dst, (slab_of(s, 1, 0), b), sends.at[4], recvs.at[4])
        for j in (1, 2, 3):
            send(src, dst, (slab_of(s, 0, j), b), sends.at[j], recvs.at[j])
        send(src, dst, twin, sends.at[8], recvs.at[8])

    def relay(ref, j, sends, recvs):
        arrived(ref, sends.at[j], recvs.at[j])
        if j == 4:
            for i in (1, 2, 3):
                send(ref, ref, (slab_of(s, 0, i), b), sends.at[4 + i], recvs.at[4 + i])
        send(ref, ref, twin, sends.at[8 + j], recvs.at[8 + j])

    spread_own(vol, planes_of(s), vs_send, vs_recv)
    spread_own(tables.at[s], tables.at[s], sl_send, sl_recv)

    for g in range(3):
        prep[g : g + 1, :] = noise[pl.ds(128 * g, 128)].reshape(1, 128)
    prep[3:128, :] = jnp.zeros((125, 128), F32)
    prep[...] = jnp.transpose(prep[...])
    vslab[:, pl.ds(pl.multiple_of(s * 16, 16), 16), :] = vol[...]
    multiply(0, 0, vol)
    build(s)

    def stored(other, dz):
        multiply(other, dz, vall.at[block(other, dz)])

    def relay_far(other):
        for side in (1, -1):
            take(other, 2, side)
            push(other, 4, side, False)
            push(other, 3, side, True)

    take_across(0, 1)
    for side in (1, -1):
        push(1, 2, side, False)
    for side in (1, -1):
        push(1, 1, side, True)
    relay_far(0)
    for side in (1, -1):
        take(0, 1, side)
        cross(1, side)
    for side in (1, -1):
        cross(2, side)
    relay(planes_of(origin_of(s, 4)), 4, vs_send, vs_recv)
    relay(tables.at[origin_of(s, 4)], 4, sl_send, sl_recv)
    stored(1, 0)
    for dz in (-1, 1, -2, 2):
        stored(0, dz)
    for j in (1, 2, 3, 5, 6, 7):
        relay(planes_of(origin_of(s, j)), j, vs_send, vs_recv)
    relay_far(1)
    for side in (1, -1):
        take(0, 3, side)
        cross(3, side)
    for side in (1, -1):
        take(0, 4, side)
    cross(4, 1)
    for side in (1, -1):
        take(1, 1, side)
        take_across(1, side)
        stored(1, -side)
    for j in range(8):
        origin = origin_of(twin_index, j)
        arrived(planes_of(origin), vs_send.at[8 + j], vs_recv.at[8 + j])

    sums = []
    for k in range(2):
        projection = dot(slices[s, 64 * k : 64 * k + 64, :], vslab[k])
        sums.append(jnp.sum(projection * projection, axis=1, keepdims=True))
    energy = jnp.concatenate(sums, axis=0)
    energy = jnp.transpose(jnp.broadcast_to(energy, (128, 128)))[0:8, :]
    eout[0] = energy
    ein[z] = energy
    for j in range(1, RING):
        send(eout.at[0], ein.at[z], (s, block(0, j)), few_send.at[0], few_recv.at[0])

    for j in (1, 2, 3, 5, 6, 7):
        relay(tables.at[origin_of(s, j)], j, sl_send, sl_recv)
    for side in (1, -1):
        stored(0, -3 * side)
        take_across(2, side)
        stored(1, -2 * side)
    stored(0, 4)
    for j in range(1, 8):
        build(origin_of(s, j))
    arrived(ein.at[pl.ds(0, RING - 1)], few_send.at[0], few_recv.at[0])
    eout[1] = jnp.sum(ein[0:RING], axis=0)
    send(eout.at[1], ein.at[RING], beside, few_send.at[1], few_recv.at[1])
    for side in (1, -1):
        take(1, 3, side)
        take_across(3, side)
        stored(1, -3 * side)
    for side in (1, -1):
        take(1, 4, side)
    take_across(4, 1)
    stored(1, 4)
    arrived(ein.at[RING], few_send.at[1], few_recv.at[1])
    energy = eout[1] + ein[RING]

    packed = jnp.concatenate(
        [acc[0:128, :], acc[128:256, :], acc[256:384, :], jnp.zeros((128, 32), F32)], axis=1
    )
    gout[:, 0:8, :] = packed.reshape(SLABS, 8, 128)
    for i in range(SLABS):
        gout[i, 8:16, :] = energy
    gin[s] = gout[s]
    for j in range(1, SLABS):
        index = lax.rem(s + j, SLABS)
        send(gout.at[index], gin.at[s], (index, b), few_send.at[2], few_recv.at[2])

    for j in range(8):
        origin = origin_of(twin_index, j)
        arrived(tables.at[origin], sl_send.at[8 + j], sl_recv.at[8 + j])
        build(origin)
    arrived(gin.at[pl.ds(0, 15)], few_send.at[2], few_recv.at[2])

    lane = lax.broadcasted_iota(jnp.int32, (8, 128), 1)
    slot = lax.div(lane, 16)
    stacked = []
    for k in range(2):
        groups = []
        for g in range(3):
            halves = []
            for upper in range(2):
                tile = jnp.zeros((8, 128), F32)
                for i in range(8):
                    shift = (16 * i - 32 * g - 16 * k) % 128
                    piece = gin[8 * upper + i, 0:8, :]
                    piece = pltpu.roll(piece, shift, 1) if shift else piece
                    tile = jnp.where(slot == i, piece, tile)
                halves.append(tile)
            groups.append(jnp.concatenate(halves, axis=1))
        stacked += in_three(jnp.concatenate(groups, axis=0))
    stacked = jnp.concatenate(stacked, axis=0).astype(BF16)

    nz = jnp.concatenate(
        [prep[pl.ds(pl.multiple_of(s * 8, 8), 8), g : g + 1] for g in range(3)], axis=0
    )
    wide_lane = lax.broadcasted_iota(jnp.int32, (24, 256), 1)
    first_class = lax.rem(wide_lane, 128) < 64
    for t in range(8):
        both = dot(stacked, slices[2 * t : 2 * t + 2].reshape(256, 256), NT)
        scores[t] = jnp.where(
            first_class,
            both[0:24] + both[24:48] + both[48:72],
            both[72:96] + both[96:120] + both[120:144],
        )
    top = None
    for t in range(8):
        energy = jnp.concatenate([gin[2 * t, 8:9, :], gin[2 * t + 1, 8:9, :]], axis=1)
        prior = jnp.concatenate([tables[2 * t, 33:34, :], tables[2 * t + 1, 33:34, :]], axis=1)
        score = nz * (scores[t] - 0.5 * energy) + prior
        scores[t] = score
        top = score if top is None else jnp.maximum(top, score)
    top = jnp.max(top, axis=1, keepdims=True)
    total = jnp.zeros((24, 256), F32)
    for t in range(8):
        total += jnp.exp(scores[t] - top)
    evidence = top + jnp.log(jnp.sum(total, axis=1, keepdims=True))
    spread = jnp.zeros((48, 256), F32)
    column = lax.broadcasted_iota(jnp.int32, (8, 128), 1)
    tile = jnp.zeros((8, 128), F32)
    for g in range(3):
        tile = jnp.where(column == g, evidence[8 * g : 8 * g + 8], tile)
    for t in range(8):
        posterior = jnp.exp(scores[t] - evidence)
        for side in range(2):
            rout[2 * t + side, 0:24, :] = posterior[:, 128 * side : 128 * side + 128]
            rout[2 * t + side, 24:32, :] = tile
        weight = jnp.concatenate(
            [jnp.where(first_class, posterior, 0.0), jnp.where(first_class, 0.0, posterior)], axis=0
        ).astype(BF16)
        spread += dot(weight, slices[2 * t : 2 * t + 2].reshape(256, 256))

    for i in range(SLABS):
        tile = jnp.zeros((8, 128), F32)
        for k in range(2):
            for g in range(3):
                at = 24 * k + 8 * g
                piece = spread[at : at + 8, 128 * (i // 8) : 128 * (i // 8) + 128]
                shift = (32 * g + 16 * k - 16 * (i % 8)) % 128
                piece = pltpu.roll(piece, shift, 1) if shift else piece
                tile = jnp.where(slot == 2 * g + k, piece, tile)
        wout[i] = tile
    win[s] = wout[s]
    for j in range(1, SLABS):
        index = lax.rem(s + j, SLABS)
        send(wout.at[index], win.at[s], (index, b), few_send.at[3], few_recv.at[3])
    arrived(win.at[pl.ds(0, 15)], few_send.at[3], few_recv.at[3])
    turned = jnp.transpose(win[...].reshape(128, 128))
    turned = jnp.concatenate([turned[0:32], turned[32:64], turned[64:96]], axis=1)
    high = turned.astype(BF16).astype(F32)
    low = turned - high
    planes = jnp.concatenate([high, low], axis=0).astype(BF16)

    def partial(other, dz):
        both = dot(planes, img[block(other, dz)])
        return both[0:rows] + both[rows : 2 * rows]

    def region(ref, other, h, side):
        ref = ref.at[16 * other + along(h, side)]
        rows_of = pl.ds(0, 16 if other else 32)
        return ref.at[rows_of, pl.ds(ends[side], half)] if h == 4 else ref.at[rows_of]

    def pass_on(value, other, h, side, near_by):
        k = 16 * other + along(h, side)
        out, into = region(red_out, other, h, side), region(red_in, other, h, side)
        if h == 4:
            value = value[:, ends[side] : ends[side] + half]
        out[...] = value.astype(BF16)
        send(out, into, (near if near_by else far)[side], red_send.at[k], red_recv.at[k])

    def pass_across(value, k, first):
        cut = pl.ds(first, 16)
        out, into = red_out.at[k].at[cut], red_in.at[k].at[cut]
        out[...] = value.astype(BF16)
        send(out, into, beside, red_send.at[k], red_recv.at[k])

    def received(k, ref):
        arrived(ref, red_send.at[k], red_recv.at[k])
        return ref[...].astype(F32)

    def came(other, h, side):
        return received(16 * other + along(h, side), region(red_in, other, h, side))

    def split(h, side):
        part = partial(1, h * side)
        pass_across(part[16:32], across(h, side), 16)
        return part[0:16]

    def joined(h, side):
        k = across(h, side)
        part = partial(0, h * side)
        extra = received(k, red_in.at[k].at[pl.ds(16, 16)])
        return jnp.concatenate([part[0:16], part[16:32] + extra], axis=0)

    def gathered(part, other, side):
        at = ends[side]
        here = part[:, at : at + half] + came(other, 4, side)
        there = part[:, half - at : width - at]
        part = jnp.concatenate([here, there] if side > 0 else [there, here], axis=1)
        return part + came(other, 3, side)

    part = split(4, 1)
    for side in (1, -1):
        pass_on(part, 1, 4, side, False)
    for side in (1, -1):
        pass_on(split(3, side), 1, 3, side, True)
    part = joined(4, 1)
    for side in (1, -1):
        pass_on(part, 0, 4, side, False)
    for side in (1, -1):
        hold[(1 - side) // 2] = split(2, side)
    for side in (1, -1):
        pass_on(joined(3, side), 0, 3, side, True)
    for side in (1, -1):
        pass_on(gathered(hold[(1 - side) // 2], 1, side), 1, 2, side, False)
    for side in (1, -1):
        pass_on(split(1, side), 1, 1, side, True)
    hold[2] = split(0, 1)
    rin[s] = rout[s]
    for j in range(1, SLABS):
        index = lax.rem(s + j, SLABS)
        send(rout.at[index], rin.at[s], (index, b), few_send.at[4], few_recv.at[4])
    for side in (1, -1):
        pass_on(gathered(joined(2, side), 0, side), 0, 2, side, False)
    for side in (1, -1):
        pass_on(joined(1, side), 0, 1, side, True)
    part = hold[2]
    for h in (1, 2):
        for side in (1, -1):
            part += came(1, h, side)
    pass_across(part, 24, 0)

    arrived(rin.at[pl.ds(0, 15)], few_send.at[4], few_recv.at[4])
    for g in range(3):
        turned = rin[:, 8 * g : 8 * g + 8, :].reshape(128, 128)
        resp_out[:, 128 * g : 128 * g + 128] = jnp.transpose(turned)
    ev_out[...] = jnp.transpose(rin[:, 24:32, :].reshape(128, 128))[0:3, :]

    part = joined(0, 1)
    for h in (1, 2):
        for side in (1, -1):
            part += came(0, h, side)
    extra = received(24, red_in.at[24].at[pl.ds(0, 16)])
    part = jnp.concatenate([part[0:16] + extra, part[16:32]], axis=0)
    for k in range(2):
        back_out[:, k, :] = part[16 * k : 16 * k + 16]

    for copy in started:
        copy.wait_send()


def local(volumes, band_weights, band_start, images, noise_precision, log_prior):
    planes, classes, width = volumes.shape
    owned = band_weights.shape[1]
    count, particles = classes * owned, images.shape[0]
    vmem = pl.BlockSpec(memory_space=pltpu.VMEM)
    dma = pltpu.SemaphoreType.DMA
    few = (SLABS, 8, 128)
    responsibilities, log_evidence, back = pl.pallas_call(
        body,
        out_shape=(
            jax.ShapeDtypeStruct((count, particles), F32),
            jax.ShapeDtypeStruct((3, 128), F32),
            jax.ShapeDtypeStruct((planes, classes, width), F32),
        ),
        in_specs=[pl.BlockSpec(memory_space=pltpu.HBM)] * 6,
        out_specs=(vmem, vmem, vmem),
        scratch_shapes=[
            pltpu.VMEM((planes, classes, width), BF16),
            pltpu.VMEM((classes, 32, owned), BF16),
            pltpu.VMEM((classes, owned), jnp.int32),
            pltpu.VMEM((classes, owned), F32),
            pltpu.VMEM((particles,), F32),
            pltpu.VMEM((BATCHES, particles, width), BF16),
            pltpu.VMEM((classes, planes, width), BF16),
            pltpu.VMEM((BATCHES, classes, planes, width), BF16),
            pltpu.VMEM((classes, SLABS * planes, width), BF16),
            pltpu.VMEM((SLABS, 40, 128), F32),
            pltpu.VMEM((SLABS, count, SLABS * planes), BF16),
            pltpu.VMEM((particles, classes * planes), F32),
            pltpu.VMEM((SLABS, 16, 128), F32),
            pltpu.VMEM((SLABS, 16, 128), F32),
            pltpu.VMEM((2, 8, 128), F32),
            pltpu.VMEM((RING + 1, 8, 128), F32),
            pltpu.VMEM((128, 128), F32),
            pltpu.VMEM((8, 24, 256), F32),
            pltpu.VMEM((SLABS, 32, 128), F32),
            pltpu.VMEM((SLABS, 32, 128), F32),
            pltpu.VMEM(few, F32),
            pltpu.VMEM(few, F32),
            pltpu.VMEM((25, 32, width), BF16),
            pltpu.VMEM((25, 32, width), BF16),
            pltpu.VMEM((3, 16, width), F32),
            dma((21,)),
            dma((24,)), dma((24,)),
            dma((16,)), dma((16,)),
            dma((16,)), dma((16,)),
            dma((5,)), dma((5,)),
            dma((25,)), dma((25,)),
        ],
        compiler_params=pltpu.CompilerParams(
            collective_id=0, has_side_effects=True, vmem_limit_bytes=48 * 1024 * 1024
        ),
    )(
        *(
            pltpu.with_memory_space_constraint(x, pltpu.MemorySpace.HBM)
            for x in (
                volumes, jnp.swapaxes(band_weights, 1, 2), band_start, log_prior,
                noise_precision, images,
            )
        )
    )
    return (
        responsibilities.reshape(classes, owned, particles),
        log_evidence.reshape(particles),
        back,
    )


def solution(mesh):
    in_specs = (
        P("slab", None, "batch"),
        P(None, "slab", None),
        P(None, "slab"),
        P("batch", None),
        P("batch"),
        P(None, "slab"),
    )
    out_specs = (P(None, "slab", "batch"), P("batch"), P("slab", None, "batch"))
    return jax.shard_map(local, mesh=mesh, in_specs=in_specs, out_specs=out_specs, check_vma=False)
```

```python
import functools

import jax
import jax.numpy as jnp
from jax import lax
from jax.experimental import pallas as pl
from jax.experimental.pallas import tpu as pltpu
from jax.sharding import PartitionSpec as P

F32, BF16 = jnp.float32, jnp.bfloat16
MESH = pl.DeviceIdType.MESH
SLABS, BATCHES, RING = 16, 16, 8
NT = (((1,), (1,)), ((), ()))
NN = (((1,), (0,)), ((), ()))


def dot(a, b, dims=NN):
    return lax.dot_general(a, b, dims, preferred_element_type=F32)


def in_three(x):
    first = x.astype(BF16).astype(F32)
    second = (x - first).astype(BF16).astype(F32)
    third = (x - first - second).astype(BF16).astype(F32)
    return first, second, third


def body(
    vol_hbm, bands_hbm, starts_hbm, priors_hbm, noise_hbm, images, resp_out, ev_out, back_out,
    vol_in, bands, starts, priors, noise, img, vol, vall, vslab, tables, slices, acc, gout, gin, eout, ein, prep,
    scores, rout, rin, wout, win, red_out, red_in, hold,
    img_sem, vb_send, vb_recv, vs_send, vs_recv, sl_send, sl_recv, few_send, few_recv,
    red_send, red_recv,
):
    s, b = lax.axis_index("slab"), lax.axis_index("batch")
    xl, z = lax.div(b, RING), lax.rem(b, RING)
    rows, width = 32, 1024
    started = []

    def block(other, dz):
        return lax.rem(xl + other, 2) * RING + lax.rem(z + dz + RING, RING)

    def send(src, dst, to, send_sem, recv_sem):
        copy = pltpu.make_async_remote_copy(
            src_ref=src, dst_ref=dst, send_sem=send_sem, recv_sem=recv_sem,
            device_id=to, device_id_type=MESH,
        )
        copy.start()
        started.append(copy)

    def arrived(ref, send_sem, recv_sem):
        pltpu.make_async_remote_copy(
            src_ref=ref, dst_ref=ref, send_sem=send_sem, recv_sem=recv_sem,
            device_id=(s, b), device_id_type=MESH,
        ).wait_recv()

    order = [(0, 0), (1, 0), (0, -1), (0, 1), (0, -2), (0, 2), (1, -1), (1, 1), (0, -3), (0, 3)]
    order += [(1, -2), (1, 2), (0, 4), (1, -3), (1, 3), (1, 4)]

    def load(i):
        at = block(*order[i])
        return pltpu.make_async_copy(
            images.at[:, pl.ds(pl.multiple_of(at * width, width), width)],
            img.at[at], img_sem.at[i],
        )

    def slab_of(index, opposite, steps):
        half_x = lax.rem(lax.div(index, 8) + opposite, 2)
        y = lax.rem(lax.div(lax.rem(index, 8), 2) + steps + 4, 4)
        return 8 * half_x + 2 * y + lax.rem(index, 2)

    twin_index = s + 1 - 2 * lax.rem(s, 2)
    barrier = pltpu.get_barrier_semaphore()
    peers = [(s, block(other, dz)) for other, dz in ((0, 1), (0, -1), (0, 2), (0, -2), (1, 0))]
    peers += [(slab_of(s, 0, j), b) for j in (1, 2, 3)]
    peers += [(slab_of(s, 1, 0), b), (twin_index, b)]
    for peer in peers:
        pl.semaphore_signal(barrier, inc=1, device_id=peer, device_id_type=MESH)

    small = [
        pltpu.make_async_copy(src, dst, img_sem.at[16 + i])
        for i, (src, dst) in enumerate(
            (
                (vol_hbm, vol_in), (bands_hbm, bands), (starts_hbm, starts),
                (priors_hbm, priors), (noise_hbm, noise),
            )
        )
    ]
    for copy in small:
        copy.start()
    for i in range(16):
        load(i).start()

    for copy in small:
        copy.wait()
    for k in range(2):
        vol[k] = vol_in[:, k, :]
    vslab[:, pl.ds(pl.multiple_of(s * 16, 16), 16), :] = vol[...]

    tables[s, 0:32, :] = jnp.concatenate([bands[0], bands[1]], axis=1).astype(F32)
    tables[s, 32:33, :] = jnp.concatenate([starts[0:1, :], starts[1:2, :]], axis=1).astype(F32)
    tables[s, 33:34, :] = jnp.concatenate([priors[0:1, :], priors[1:2, :]], axis=1)
    tables[s, 34:40, :] = jnp.zeros((6, 128), F32)

    plane = lax.broadcasted_iota(jnp.int32, (128, 128), 1).astype(F32)

    def build(index):
        table = jnp.concatenate([tables[index], jnp.zeros((88, 128), F32)], axis=0)
        moved = jnp.transpose(table)
        start = jnp.broadcast_to(moved[:, 32:33], (128, 128))
        rest = jnp.where(start >= 128.0, start - 128.0, start)
        for step in (64, 32, 16, 8, 4, 2, 1):
            hit = rest >= float(step)
            moved = jnp.where(hit, pltpu.roll(moved, step, 1), moved)
            rest = jnp.where(hit, rest - float(step), rest)
        parts = []
        for first in (0.0, 128.0):
            offset = plane + first - start
            inside = jnp.logical_and(offset >= 0.0, offset < 32.0)
            parts.append(jnp.where(inside, moved, 0.0))
        slices[index] = jnp.concatenate(parts, axis=1).astype(BF16)

    def multiply(other, dz, ref):
        i = order.index((other, dz))
        load(i).wait()
        part = dot(img[block(other, dz)], ref[...].reshape(rows, width), NT)
        if i == 0:
            acc[...] = part
        else:
            acc[...] += part

    pl.semaphore_wait(barrier, 10)

    right = (s, block(0, 1))
    left = (s, block(0, -1))
    beside = (s, block(1, 0))
    twin_index = s + 1 - 2 * lax.rem(s, 2)
    twin = (twin_index, b)

    half = width // 2
    ends = {1: 0, -1: half}

    near = {1: right, -1: left}
    far = {1: (s, block(0, 2)), -1: (s, block(0, -2))}

    def along(h, side):
        return 2 * (h - 1) + (side < 0)

    def across(h, side):
        return 8 if h == 0 else 7 + 2 * h + (side < 0)

    def part_of(other, ref):
        return ref.at[pl.ds(0, 1)] if other else ref

    def push(other, h, side, near_by, src=None):
        dst = vall.at[block(other, -side * (h - (1 if near_by else 2)))]
        src = part_of(other, dst if src is None else src)
        dst = part_of(other, dst)
        if h == 4:
            cut = pl.ds(ends[side], half)
            src, dst = src.at[:, :, cut], dst.at[:, :, cut]
        k = 16 * other + along(h, side)
        send(src, dst, (near if near_by else far)[side], vb_send.at[k], vb_recv.at[k])

    def take(other, h, side):
        ref = part_of(other, vall.at[block(other, -h * side)])
        if h == 4:
            ref = ref.at[:, :, pl.ds(ends[side], half)]
        k = 16 * other + along(h, side)
        arrived(ref, vb_send.at[k], vb_recv.at[k])

    def cross(h, side, src=None):
        k = across(h, side)
        dst = vall.at[block(0, -h * side)]
        src = dst if src is None else src
        if h:
            src, dst = src.at[pl.ds(1, 1)], dst.at[pl.ds(1, 1)]
        send(src, dst, beside, vb_send.at[k], vb_recv.at[k])

    def take_across(h, side):
        k = across(h, side)
        ref = vall.at[block(1, -h * side)]
        if h:
            ref = ref.at[pl.ds(1, 1)]
        arrived(ref, vb_send.at[k], vb_recv.at[k])

    for side in (1, -1):
        push(0, 2, side, False, vol)
    cross(0, 1, vol)
    for side in (1, -1):
        push(0, 1, side, True, vol)

    def planes_of(index):
        return vslab.at[:, pl.ds(pl.multiple_of(index * 16, 16), 16), :]

    def origin_of(index, j):
        return slab_of(index, 1, 4 - j) if j >= 4 else slab_of(index, 0, -j)

    def spread_own(src, dst, sends, recvs):
        send(src, dst, (slab_of(s, 1, 0), b), sends.at[4], recvs.at[4])
        for j in (1, 2, 3):
            send(src, dst, (slab_of(s, 0, j), b), sends.at[j], recvs.at[j])
        send(src, dst, twin, sends.at[8], recvs.at[8])

    def relay(ref, j, sends, recvs):
        arrived(ref, sends.at[j], recvs.at[j])
        if j == 4:
            for i in (1, 2, 3):
                send(ref, ref, (slab_of(s, 0, i), b), sends.at[4 + i], recvs.at[4 + i])
        send(ref, ref, twin, sends.at[8 + j], recvs.at[8 + j])

    spread_own(vol, planes_of(s), vs_send, vs_recv)
    spread_own(tables.at[s], tables.at[s], sl_send, sl_recv)

    for g in range(3):
        prep[g : g + 1, :] = noise[pl.ds(128 * g, 128)].reshape(1, 128)
    prep[3:128, :] = jnp.zeros((125, 128), F32)
    prep[...] = jnp.transpose(prep[...])
    vslab[:, pl.ds(pl.multiple_of(s * 16, 16), 16), :] = vol[...]
    multiply(0, 0, vol)
    build(s)

    def stored(other, dz):
        multiply(other, dz, vall.at[block(other, dz)])

    def relay_far(other):
        for side in (1, -1):
            take(other, 2, side)
            push(other, 4, side, False)
            push(other, 3, side, True)

    take_across(0, 1)
    for side in (1, -1):
        push(1, 2, side, False)
    for side in (1, -1):
        push(1, 1, side, True)
    relay_far(0)
    for side in (1, -1):
        take(0, 1, side)
        cross(1, side)
    for side in (1, -1):
        cross(2, side)
    relay(planes_of(origin_of(s, 4)), 4, vs_send, vs_recv)
    relay(tables.at[origin_of(s, 4)], 4, sl_send, sl_recv)
    stored(1, 0)
    for dz in (-1, 1, -2, 2):
        stored(0, dz)
    for j in (1, 2, 3, 5, 6, 7):
        relay(planes_of(origin_of(s, j)), j, vs_send, vs_recv)
    relay_far(1)
    for side in (1, -1):
        take(0, 3, side)
        cross(3, side)
    for side in (1, -1):
        take(0, 4, side)
    cross(4, 1)
    for side in (1, -1):
        take(1, 1, side)
        take_across(1, side)
        stored(1, -side)
    for j in range(8):
        origin = origin_of(twin_index, j)
        arrived(planes_of(origin), vs_send.at[8 + j], vs_recv.at[8 + j])

    sums = []
    for k in range(2):
        projection = dot(slices[s, 64 * k : 64 * k + 64, :], vslab[k])
        sums.append(jnp.sum(projection * projection, axis=1, keepdims=True))
    energy = jnp.concatenate(sums, axis=0)
    energy = jnp.transpose(jnp.broadcast_to(energy, (128, 128)))[0:8, :]
    eout[0] = energy
    ein[z] = energy
    for j in range(1, RING):
        send(eout.at[0], ein.at[z], (s, block(0, j)), few_send.at[0], few_recv.at[0])

    for j in (1, 2, 3, 5, 6, 7):
        relay(tables.at[origin_of(s, j)], j, sl_send, sl_recv)
    for side in (1, -1):
        stored(0, -3 * side)
        take_across(2, side)
        stored(1, -2 * side)
    stored(0, 4)
    for j in range(1, 8):
        build(origin_of(s, j))
    arrived(ein.at[pl.ds(0, RING - 1)], few_send.at[0], few_recv.at[0])
    eout[1] = jnp.sum(ein[0:RING], axis=0)
    send(eout.at[1], ein.at[RING], beside, few_send.at[1], few_recv.at[1])
    for side in (1, -1):
        take(1, 3, side)
        take_across(3, side)
        stored(1, -3 * side)
    for side in (1, -1):
        take(1, 4, side)
    take_across(4, 1)
    stored(1, 4)
    arrived(ein.at[RING], few_send.at[1], few_recv.at[1])
    energy = eout[1] + ein[RING]

    packed = jnp.concatenate(
        [acc[0:128, :], acc[128:256, :], acc[256:384, :], jnp.zeros((128, 32), F32)], axis=1
    )
    gout[:, 0:8, :] = packed.reshape(SLABS, 8, 128)
    for i in range(SLABS):
        gout[i, 8:16, :] = energy
    gin[s] = gout[s]
    for j in range(1, SLABS):
        index = lax.rem(s + j, SLABS)
        send(gout.at[index], gin.at[s], (index, b), few_send.at[2], few_recv.at[2])

    for j in range(8):
        origin = origin_of(twin_index, j)
        arrived(tables.at[origin], sl_send.at[8 + j], sl_recv.at[8 + j])
        build(origin)
    arrived(gin.at[pl.ds(0, 15)], few_send.at[2], few_recv.at[2])

    lane = lax.broadcasted_iota(jnp.int32, (8, 128), 1)
    slot = lax.div(lane, 16)
    stacked = []
    for k in range(2):
        groups = []
        for g in range(3):
            halves = []
            for upper in range(2):
                tile = jnp.zeros((8, 128), F32)
                for i in range(8):
                    shift = (16 * i - 32 * g - 16 * k) % 128
                    piece = gin[8 * upper + i, 0:8, :]
                    piece = pltpu.roll(piece, shift, 1) if shift else piece
                    tile = jnp.where(slot == i, piece, tile)
                halves.append(tile)
            groups.append(jnp.concatenate(halves, axis=1))
        stacked += in_three(jnp.concatenate(groups, axis=0))
    stacked = jnp.concatenate(stacked, axis=0).astype(BF16)

    nz = jnp.concatenate(
        [prep[pl.ds(pl.multiple_of(s * 8, 8), 8), g : g + 1] for g in range(3)], axis=0
    )
    wide_lane = lax.broadcasted_iota(jnp.int32, (24, 256), 1)
    first_class = lax.rem(wide_lane, 128) < 64
    for t in range(8):
        both = dot(stacked, slices[2 * t : 2 * t + 2].reshape(256, 256), NT)
        scores[t] = jnp.where(
            first_class,
            both[0:24] + both[24:48] + both[48:72],
            both[72:96] + both[96:120] + both[120:144],
        )
    top = None
    for t in range(8):
        energy = jnp.concatenate([gin[2 * t, 8:9, :], gin[2 * t + 1, 8:9, :]], axis=1)
        prior = jnp.concatenate([tables[2 * t, 33:34, :], tables[2 * t + 1, 33:34, :]], axis=1)
        score = nz * (scores[t] - 0.5 * energy) + prior
        scores[t] = score
        top = score if top is None else jnp.maximum(top, score)
    top = jnp.max(top, axis=1, keepdims=True)
    total = jnp.zeros((24, 256), F32)
    for t in range(8):
        total += jnp.exp(scores[t] - top)
    evidence = top + jnp.log(jnp.sum(total, axis=1, keepdims=True))
    spread = jnp.zeros((48, 256), F32)
    column = lax.broadcasted_iota(jnp.int32, (8, 128), 1)
    tile = jnp.zeros((8, 128), F32)
    for g in range(3):
        tile = jnp.where(column == g, evidence[8 * g : 8 * g + 8], tile)
    for t in range(8):
        posterior = jnp.exp(scores[t] - evidence)
        for side in range(2):
            rout[2 * t + side, 0:24, :] = posterior[:, 128 * side : 128 * side + 128]
            rout[2 * t + side, 24:32, :] = tile
        weight = jnp.concatenate(
            [jnp.where(first_class, posterior, 0.0), jnp.where(first_class, 0.0, posterior)], axis=0
        ).astype(BF16)
        spread += dot(weight, slices[2 * t : 2 * t + 2].reshape(256, 256))

    for i in range(SLABS):
        tile = jnp.zeros((8, 128), F32)
        for k in range(2):
            for g in range(3):
                at = 24 * k + 8 * g
                piece = spread[at : at + 8, 128 * (i // 8) : 128 * (i // 8) + 128]
                shift = (32 * g + 16 * k - 16 * (i % 8)) % 128
                piece = pltpu.roll(piece, shift, 1) if shift else piece
                tile = jnp.where(slot == 2 * g + k, piece, tile)
        wout[i] = tile
    win[s] = wout[s]
    for j in range(1, SLABS):
        index = lax.rem(s + j, SLABS)
        send(wout.at[index], win.at[s], (index, b), few_send.at[3], few_recv.at[3])
    arrived(win.at[pl.ds(0, 15)], few_send.at[3], few_recv.at[3])
    turned = jnp.transpose(win[...].reshape(128, 128))
    turned = jnp.concatenate([turned[0:32], turned[32:64], turned[64:96]], axis=1)
    high = turned.astype(BF16).astype(F32)
    low = turned - high
    planes = jnp.concatenate([high, low], axis=0).astype(BF16)

    def partial(other, dz):
        both = dot(planes, img[block(other, dz)])
        return both[0:rows] + both[rows : 2 * rows]

    def region(ref, other, h, side):
        ref = ref.at[16 * other + along(h, side)]
        rows_of = pl.ds(0, 16 if other else 32)
        return ref.at[rows_of, pl.ds(ends[side], half)] if h == 4 else ref.at[rows_of]

    def pass_on(value, other, h, side, near_by):
        k = 16 * other + along(h, side)
        out, into = region(red_out, other, h, side), region(red_in, other, h, side)
        if h == 4:
            value = value[:, ends[side] : ends[side] + half]
        out[...] = value.astype(BF16)
        send(out, into, (near if near_by else far)[side], red_send.at[k], red_recv.at[k])

    def pass_across(value, k, first):
        cut = pl.ds(first, 16)
        out, into = red_out.at[k].at[cut], red_in.at[k].at[cut]
        out[...] = value.astype(BF16)
        send(out, into, beside, red_send.at[k], red_recv.at[k])

    def received(k, ref):
        arrived(ref, red_send.at[k], red_recv.at[k])
        return ref[...].astype(F32)

    def came(other, h, side):
        return received(16 * other + along(h, side), region(red_in, other, h, side))

    def split(h, side):
        part = partial(1, h * side)
        pass_across(part[16:32], across(h, side), 16)
        return part[0:16]

    def joined(h, side):
        k = across(h, side)
        part = partial(0, h * side)
        extra = received(k, red_in.at[k].at[pl.ds(16, 16)])
        return jnp.concatenate([part[0:16], part[16:32] + extra], axis=0)

    def gathered(part, other, side):
        at = ends[side]
        here = part[:, at : at + half] + came(other, 4, side)
        there = part[:, half - at : width - at]
        part = jnp.concatenate([here, there] if side > 0 else [there, here], axis=1)
        return part + came(other, 3, side)

    part = split(4, 1)
    for side in (1, -1):
        pass_on(part, 1, 4, side, False)
    for side in (1, -1):
        pass_on(split(3, side), 1, 3, side, True)
    part = joined(4, 1)
    for side in (1, -1):
        pass_on(part, 0, 4, side, False)
    for side in (1, -1):
        hold[(1 - side) // 2] = split(2, side)
    for side in (1, -1):
        pass_on(joined(3, side), 0, 3, side, True)
    for side in (1, -1):
        pass_on(gathered(hold[(1 - side) // 2], 1, side), 1, 2, side, False)
    for side in (1, -1):
        pass_on(split(1, side), 1, 1, side, True)
    hold[2] = split(0, 1)
    rin[s] = rout[s]
    for j in range(1, SLABS):
        index = lax.rem(s + j, SLABS)
        send(rout.at[index], rin.at[s], (index, b), few_send.at[4], few_recv.at[4])
    for side in (1, -1):
        pass_on(gathered(joined(2, side), 0, side), 0, 2, side, False)
    for side in (1, -1):
        pass_on(joined(1, side), 0, 1, side, True)
    part = hold[2]
    for h in (1, 2):
        for side in (1, -1):
            part += came(1, h, side)
    pass_across(part, 24, 0)

    arrived(rin.at[pl.ds(0, 15)], few_send.at[4], few_recv.at[4])
    for g in range(3):
        turned = rin[:, 8 * g : 8 * g + 8, :].reshape(128, 128)
        resp_out[:, 128 * g : 128 * g + 128] = jnp.transpose(turned)
    ev_out[...] = jnp.transpose(rin[:, 24:32, :].reshape(128, 128))[0:3, :]

    part = joined(0, 1)
    for h in (1, 2):
        for side in (1, -1):
            part += came(0, h, side)
    extra = received(24, red_in.at[24].at[pl.ds(0, 16)])
    part = jnp.concatenate([part[0:16] + extra, part[16:32]], axis=0)
    for k in range(2):
        back_out[:, k, :] = part[16 * k : 16 * k + 16]

    for copy in started:
        copy.wait_send()


def local(volumes, band_weights, band_start, images, noise_precision, log_prior):
    planes, classes, width = volumes.shape
    owned = band_weights.shape[1]
    count, particles = classes * owned, images.shape[0]
    vmem = pl.BlockSpec(memory_space=pltpu.VMEM)
    dma = pltpu.SemaphoreType.DMA
    few = (SLABS, 8, 128)
    responsibilities, log_evidence, back = pl.pallas_call(
        body,
        out_shape=(
            jax.ShapeDtypeStruct((count, particles), F32),
            jax.ShapeDtypeStruct((3, 128), F32),
            jax.ShapeDtypeStruct((planes, classes, width), F32),
        ),
        in_specs=[pl.BlockSpec(memory_space=pltpu.HBM)] * 6,
        out_specs=(vmem, vmem, vmem),
        scratch_shapes=[
            pltpu.VMEM((planes, classes, width), BF16),
            pltpu.VMEM((classes, 32, owned), BF16),
            pltpu.VMEM((classes, owned), jnp.int32),
            pltpu.VMEM((classes, owned), F32),
            pltpu.VMEM((particles,), F32),
            pltpu.VMEM((BATCHES, particles, width), BF16),
            pltpu.VMEM((classes, planes, width), BF16),
            pltpu.VMEM((BATCHES, classes, planes, width), BF16),
            pltpu.VMEM((classes, SLABS * planes, width), BF16),
            pltpu.VMEM((SLABS, 40, 128), F32),
            pltpu.VMEM((SLABS, count, SLABS * planes), BF16),
            pltpu.VMEM((particles, classes * planes), F32),
            pltpu.VMEM((SLABS, 16, 128), F32),
            pltpu.VMEM((SLABS, 16, 128), F32),
            pltpu.VMEM((2, 8, 128), F32),
            pltpu.VMEM((RING + 1, 8, 128), F32),
            pltpu.VMEM((128, 128), F32),
            pltpu.VMEM((8, 24, 256), F32),
            pltpu.VMEM((SLABS, 32, 128), F32),
            pltpu.VMEM((SLABS, 32, 128), F32),
            pltpu.VMEM(few, F32),
            pltpu.VMEM(few, F32),
            pltpu.VMEM((25, 32, width), BF16),
            pltpu.VMEM((25, 32, width), BF16),
            pltpu.VMEM((3, 16, width), F32),
            dma((21,)),
            dma((24,)), dma((24,)),
            dma((16,)), dma((16,)),
            dma((16,)), dma((16,)),
            dma((5,)), dma((5,)),
            dma((25,)), dma((25,)),
        ],
        compiler_params=pltpu.CompilerParams(
            collective_id=0, has_side_effects=True, vmem_limit_bytes=48 * 1024 * 1024
        ),
    )(
        *(
            pltpu.with_memory_space_constraint(x, pltpu.MemorySpace.HBM)
            for x in (
                volumes, jnp.swapaxes(band_weights, 1, 2), band_start, log_prior,
                noise_precision, images,
            )
        )
    )
    return (
        responsibilities.reshape(classes, owned, particles),
        log_evidence.reshape(particles),
        back,
    )


def solution(mesh):
    in_specs = (
        P("slab", None, "batch"),
        P(None, "slab", None),
        P(None, "slab"),
        P("batch", None),
        P("batch"),
        P(None, "slab"),
    )
    out_specs = (P(None, "slab", "batch"), P("batch"), P("slab", None, "batch"))
    return jax.shard_map(local, mesh=mesh, in_specs=in_specs, out_specs=out_specs, check_vma=False)
```
